32 devices in a mesh: grp: 4 (over x, core), rep: 8 (over z, y).
Axes of the slice: x: 2, y: 2, z: 4, core: 2. Of those that a mesh axis runs over, the one named last changes fastest.
Arguments:
- tokens: bfloat16 [128, 1024, 576], P(('grp', 'rep')), may hold values from -6 to 6
- attention_gain: bfloat16 [576], replicated, may hold values from 0.099609375 to 1.8984375
- query_weight: bfloat16 [576, 576], replicated, may hold values from -0.25 to 0.25
- key_weight: bfloat16 [576, 192], replicated, may hold values from -0.25 to 0.25
- value_weight: bfloat16 [576, 192], replicated, may hold values from -0.25 to 0.25
- output_weight: bfloat16 [576, 576], replicated, may hold values from -0.75 to 0.75
- feed_gain: bfloat16 [576], replicated, may hold values from 0.099609375 to 1.8984375
- gate_weight: bfloat16 [576, 1536], replicated, may hold values from -0.25 to 0.25
- up_weight: bfloat16 [576, 1536], replicated, may hold values from -0.25 to 0.25
- down_weight: bfloat16 [1536, 576], replicated, may hold values from -0.21875 to 0.21875
- router: bfloat16 [3, 576], replicated, may hold values from -0.1875 to 0.1875
- out_grad: bfloat16 [128, 1024, 576], P(('grp', 'rep')), may hold values from -6 to 6
- doc_lengths: int32 [4, 32, 4], P(None, 'rep'), may hold values from 1 to 512, 1024 in all within a row
- picks_first: int32 [4, 32, 192], P(None, 'rep'), may hold values from 0 to 1023, as said below
- picks_second: int32 [4, 32, 96], P(None, 'rep'), may hold values from 0 to 1023, as said below
- picks_third: int32 [4, 32, 48], P(None, 'rep'), may hold values from 0 to 1023, as said below
- routes: int32 [4, 32, 3, 2], P(None, 'rep'), may hold values from 0 to 192, as said below
Outputs:
- out_state: bfloat16 [128, 1024, 576], P(('grp', 'rep'))
- grad_tokens: bfloat16 [128, 1024, 576], P(('grp', 'rep'))
- grad_attention_gain: float32 [576], replicated
- grad_query_weight: float32 [576, 576], replicated
- grad_key_weight: float32 [576, 192], replicated
- grad_value_weight: float32 [576, 192], replicated
- grad_output_weight: float32 [576, 576], replicated
- grad_feed_gain: float32 [576], replicated
- grad_gate_weight: float32 [576, 1536], replicated
- grad_up_weight: float32 [576, 1536], replicated
- grad_down_weight: float32 [1536, 576], replicated
- grad_router: float32 [3, 576], replicated
The draws below stay inside these ranges and needn't reach their ends.
Inputs may be any that keep to these rules, and one draw needn't show every extreme that they name: routes[i, c, r, 0] is the count of picked tokens of that sequence at recursion r + 1: from 64 to 192 at the first, 32 to 96 at the second, 16 to 48 at the third, never rising from one recursion to the next, each largest count present in every draw. routes[i, c, r, 1] is the sequence's bucket, a grp index; the sequences of one device go to different buckets, and every bucket receives exactly 512, 256, 128 picked tokens at recursions 1, 2, 3. `picks_first`: the first count entries of a row are distinct positions in rising order, the rest 0; a recursion's picked tokens are among the previous recursion's. `picks_second`: as picks_first, for recursion 2. `picks_third`: as picks_first, for recursion 3. `doc_lengths`: each row sums to 1024.
All inputs are finite; a program needn't handle non-finite values.
Results may differ from the reference program's by a relative error of at most 0.03.
Values may be sent and summed in bfloat16 or wider, within the bound.
A program may use at most 448 MiB of HBM per device.

```python
import math
import jax
import jax.numpy as jnp
import numpy as np
from jax import lax

D = 576
HEADS = 9
KV_HEADS = 3
HEAD_DIM = 64
FF = 1536
NREC = 3
SEQ = 1024
NDOC = 4
UNIT = 16
DOC_MOST = 512
BUCKETS = 4
TEAMS = 8
SEQS_DEV = 4
SEQS_GRP = 32
SEQS = 128
SLOT1 = 192
SLOT2 = 96
SLOT3 = 48


def route_plan(key):
    members = SEQS_DEV
    pair_count = members // 2
    unit_sizes = [UNIT * 2 ** (NREC - 1 - recursion) for recursion in range(NREC)]
    offset_key = jax.random.fold_in(key, 11)
    offsets = jax.vmap(lambda team_key: jax.random.permutation(team_key, BUCKETS)[:members])(jax.random.split(offset_key, TEAMS))
    force_key = jax.random.fold_in(key, 12)
    forced_group = jax.random.randint(force_key, (TEAMS,), 0, BUCKETS)
    forced = (jnp.arange(BUCKETS)[None, :, None] == forced_group[:, None, None]) & (jnp.arange(pair_count)[None, None, :] == 0)
    swing_shape = (TEAMS, BUCKETS, pair_count)
    swings = []
    previous = None
    for recursion in range(NREC):
        unit_now = unit_sizes[recursion]
        swing_key = jax.random.fold_in(key, 20 + recursion)
        if previous is None:
            lower_end = jnp.full(swing_shape, -unit_now, jnp.int32)
            upper_end = jnp.full(swing_shape, unit_now, jnp.int32)
        else:
            lower_end = jnp.maximum(-unit_now, previous - 2 * unit_now)
            upper_end = jnp.minimum(unit_now, previous + 2 * unit_now)
        drawn_now = jax.random.randint(swing_key, swing_shape, lower_end, upper_end + 1)
        drawn_now = jnp.where(forced, unit_now, drawn_now).astype(jnp.int32)
        swings.append(drawn_now)
        previous = drawn_now
    bucket_ids = jnp.arange(BUCKETS)[:, None, None]
    team_ids = jnp.arange(TEAMS)[None, :, None]
    member_ids = jnp.arange(members)[None, None, :]
    quota_group = (bucket_ids + offsets[None, :, :]) % BUCKETS
    sign_of = 1 - 2 * (member_ids % 2)
    count_list = []
    bucket_list = []
    order_key = jax.random.fold_in(key, 30)
    for recursion in range(NREC):
        picked = swings[recursion][team_ids, quota_group, member_ids // 2]
        count_list.append(2 * unit_sizes[recursion] + sign_of * picked)
        orders = jax.vmap(lambda team_key: jax.random.permutation(team_key, BUCKETS))(jax.random.split(jax.random.fold_in(order_key, recursion), TEAMS))
        bucket_list.append(orders[team_ids, quota_group])
    counts = jnp.stack(count_list, -1).reshape(BUCKETS, SEQS_GRP, NREC).astype(jnp.int32)
    buckets = jnp.stack(bucket_list, -1).reshape(BUCKETS, SEQS_GRP, NREC).astype(jnp.int32)
    return (counts, buckets)


def active_positions(key, recursion, width_now):
    counts = route_plan(key)[0][:, :, recursion].reshape(SEQS)
    rank_key = jax.random.fold_in(key, 40)
    ranks = jax.vmap(lambda seq_key: jax.random.permutation(seq_key, SEQ))(jax.random.split(rank_key, SEQS))
    positions = jnp.arange(SEQ)[None, :]
    chosen = ranks < counts[:, None]
    ordering = jnp.argsort(jnp.where(chosen, positions, SEQ + positions), axis=-1)[:, :width_now]
    column = jnp.arange(width_now)[None, :]
    picked = jnp.where(column < counts[:, None], ordering, 0).astype(jnp.int32)
    return picked.reshape(BUCKETS, SEQS_GRP, width_now)


def draw_routes(key, part):
    counts, buckets = route_plan(key)
    return jnp.stack([counts, buckets], -1)


def draw_picks_first(key, part):
    return active_positions(key, 0, SLOT1)


def draw_picks_second(key, part):
    return active_positions(key, 1, SLOT2)


def draw_picks_third(key, part):
    return active_positions(key, 2, SLOT3)


def steps_of(key, dims, cuts, least, high):
    loudness, own = 1.0, jax.random.fold_in(key, 6)
    for axis_at, blocks in cuts:
        draws = jnp.exp(jax.random.uniform(jax.random.fold_in(own, axis_at), (blocks,), jnp.float32, least / len(cuts), high / len(cuts)))
        loudness = loudness * jnp.repeat(draws, dims[axis_at] // blocks).reshape([-1 if axis == axis_at else 1 for axis in range(len(dims))])
    return loudness


def length_profile(number_of, total, reach, lean):
    portions = [(1 << 20) // math.isqrt(rank ** lean) + 1 for rank in range(2, number_of + 1)]
    rest, given = total - reach - (number_of - 1), [1] * (number_of - 1)
    while rest > 0:
        movable = [i for i in range(number_of - 1) if given[i] < reach]
        mass, remaining = sum([portions[i] for i in movable]), rest
        for i in movable:
            addition = min(reach - given[i], max(1, remaining * portions[i] // mass), rest)
            given[i] = given[i] + addition
            rest = rest - addition
    return np.array([reach] + given)


def uneven_parts(key, amount, total, most, slope):
    if amount == 2:
        one = jax.random.randint(key, (), max(1, total - most), min(most, total - 1) + 1)
        return jnp.stack([one, total - one])
    tallies = jnp.asarray(length_profile(amount, total, most, slope), jnp.int32)
    twos = (amount - 1) // 2
    donor, taker = tallies[1:1 + 2 * twos:2], tallies[2:2 + 2 * twos:2]
    slack = jnp.minimum(donor - 1, most - taker)
    moved = jax.random.randint(jax.random.fold_in(key, 1), (twos,), 0, 1 << 20) % (slack + 1)
    tallies = tallies.at[1:1 + 2 * twos:2].set(donor - moved).at[2:2 + 2 * twos:2].set(taker + moved)
    return tallies[jax.random.permutation(jax.random.fold_in(key, 2), amount)]


def centred(own_key, dims, scale, bound, cuts=(), kind=jnp.bfloat16):
    drawn = jax.random.normal(own_key, dims, jnp.float32) * scale
    if len(cuts) > 0:
        drawn = steps_of(own_key, dims, cuts, -0.22, 0.18) * drawn
    return jnp.clip(drawn, min=-bound, max=bound).astype(kind)


def setup_inputs(seed: int = 0) -> dict:
    arg_keys = jax.random.split(jax.random.key(seed), 18)
    return {
        "tokens": centred(arg_keys[0], (SEQS, SEQ, D), 1.0, 6.0, ((0, 32),)),
        "attention_gain": jnp.clip(1.0 + 0.18 * jax.random.normal(arg_keys[1], (D,), jnp.float32), 0.099609375, 1.8984375).astype(jnp.bfloat16),
        "query_weight": centred(arg_keys[2], (D, D), D ** -0.5, 0.25),
        "key_weight": centred(arg_keys[3], (D, KV_HEADS * HEAD_DIM), D ** -0.5, 0.25),
        "value_weight": centred(arg_keys[4], (D, KV_HEADS * HEAD_DIM), D ** -0.5, 0.25),
        "output_weight": centred(arg_keys[5], (D, D), (D // 8) ** -0.5, 0.75),
        "feed_gain": jnp.clip(1.0 + 0.18 * jax.random.normal(arg_keys[6], (D,), jnp.float32), 0.099609375, 1.8984375).astype(jnp.bfloat16),
        "gate_weight": centred(arg_keys[7], (D, FF), D ** -0.5, 0.25),
        "up_weight": centred(arg_keys[8], (D, FF), D ** -0.5, 0.25),
        "down_weight": centred(arg_keys[9], (FF, D), (FF // 2) ** -0.5, 0.21875),
        "router": centred(arg_keys[10], (NREC, D), (2 * D) ** -0.5, 0.1875),
        "out_grad": centred(arg_keys[11], (SEQS, SEQ, D), 1.0, 6.0, ((0, 32),)),
        "doc_lengths": jax.vmap(lambda own: uneven_parts(own, NDOC, SEQ, DOC_MOST, 2))(jax.random.split(arg_keys[12], BUCKETS * SEQS_GRP)).reshape((BUCKETS, SEQS_GRP, NDOC)).astype(jnp.int32),
        "picks_first": draw_picks_first(jax.random.fold_in(arg_keys[17], 71), 0),
        "picks_second": draw_picks_second(jax.random.fold_in(arg_keys[17], 71), 0),
        "picks_third": draw_picks_third(jax.random.fold_in(arg_keys[17], 71), 0),
        "routes": draw_routes(jax.random.fold_in(arg_keys[17], 71), 0),
    }


EPSILON = 1e-05
ROPE_BASE = 10000.0
SCORE_SCALE = 0.125
MASKED = -1e+30
PRECISE = lax.Precision.HIGHEST

@jax.custom_vjp
def low(v):
    return lax.optimization_barrier(v.astype(jnp.bfloat16)).astype(jnp.float32)

@jax.custom_vjp
def low_back(v):
    return v

def low_keep(v):
    return (low(v), None)

def low_pass(kept, grad):
    return (grad,)

def back_keep(v):
    return (v, None)

def back_low(kept, grad):
    return (low(grad),)
low.defvjp(low_keep, low_pass)
low_back.defvjp(back_keep, back_low)

def rms_scale(values):
    return lax.rsqrt(lax.optimization_barrier(jnp.mean(values * values, axis=-1, keepdims=True)) + EPSILON)

def rope_tables(positions):
    halfway = HEAD_DIM // 2
    inverse = ROPE_BASE ** (-(jnp.arange(halfway, dtype=jnp.float32) * (2.0 / HEAD_DIM)))
    angles = positions.astype(jnp.float32)[..., None] * inverse
    cosines = jnp.cos(angles)
    sine_values = jnp.sin(angles)
    return (jnp.concatenate([cosines, cosines], -1), jnp.concatenate([sine_values, sine_values], -1))

def rotate(values, cosines, sine_values):
    halfway = values.shape[-1] // 2
    turned = jnp.concatenate([-values[..., halfway:], values[..., :halfway]], -1)
    return values * cosines + turned * sine_values

def attention_mask(labels, starts, positions, active):
    same_doc = (labels[:, :, None] == labels[:, None, :]) & (starts[:, :, None] == starts[:, None, :])
    causal = positions[:, None, :] <= positions[:, :, None]
    length = labels.shape[1]
    return same_doc & causal & active[:, None, :] | jnp.eye(length, dtype=bool)[None]

def block_rows(sent, allowed, positions, params):
    attention_gain, query_weight, key_weight, value_weight, output_weight, feed_gain, gate_weight, up_weight, down_weight = params
    group_count, length, model_width = sent.shape
    per_group = HEADS // KV_HEADS
    flat_rows = sent.reshape(group_count * length, model_width)
    normed_one = low(flat_rows * rms_scale(flat_rows) * attention_gain)
    query_rows = low_back(jnp.dot(normed_one, query_weight, precision=PRECISE)).reshape(group_count, length, KV_HEADS, per_group, HEAD_DIM)
    key_pre = low_back(jnp.dot(normed_one, key_weight, precision=PRECISE)).reshape(group_count, length, KV_HEADS, HEAD_DIM)
    value_low = low(low_back(jnp.dot(normed_one, value_weight, precision=PRECISE))).reshape(group_count, length, KV_HEADS, HEAD_DIM)
    cosines, sine_values = rope_tables(positions)
    query_low = low(rotate(query_rows, cosines[:, :, None, None], sine_values[:, :, None, None]))
    key_low = low(rotate(key_pre, cosines[:, :, None], sine_values[:, :, None]))
    scores = low_back(jnp.einsum('gqkhd,gskd->gkhqs', query_low, key_low, precision=PRECISE) * SCORE_SCALE)
    scores = jnp.where(allowed[:, None, None], scores, MASKED)
    shares = jnp.exp(scores - jax.nn.logsumexp(scores, axis=-1, keepdims=True))
    mixed_rows = jnp.einsum('gkhqs,gskd->gqkhd', low(shares), value_low, precision=PRECISE)
    mixed_low = low(low_back(mixed_rows.reshape(group_count * length, model_width)))
    attended = low_back(jnp.dot(mixed_low, output_weight, precision=PRECISE))
    middle = flat_rows + attended
    normed_two = low(middle * rms_scale(middle) * feed_gain)
    gate_pre = low_back(jnp.dot(normed_two, gate_weight, precision=PRECISE))
    up_pre = low_back(jnp.dot(normed_two, up_weight, precision=PRECISE))
    hidden = low(jax.nn.silu(gate_pre) * up_pre)
    change = attended + jnp.dot(hidden, down_weight, precision=PRECISE)
    return change.reshape(group_count, length, model_width)

def forward(params, router_rows, residual, layouts):
    for recursion in range(NREC):
        pick_list, active, starts = layouts[recursion]
        slot_count = pick_list.shape[1]
        picked_rows = jax.vmap(lambda whole_seq, where_at: whole_seq[where_at])(residual, pick_list)
        gate_values = jax.nn.sigmoid(lax.optimization_barrier(jnp.sum(picked_rows * router_rows[recursion], axis=-1)))
        sent = low_back(low(picked_rows))
        batches = SEQS // SEQS_DEV

        def one_batch(pieces):
            rows_part, starts_part, picks_part, active_part = pieces
            allowed = attention_mask(jnp.zeros_like(picks_part), starts_part, picks_part, active_part)
            return block_rows(rows_part, allowed, picks_part, params)
        change = lax.map(jax.checkpoint(one_batch), (sent.reshape(batches, SEQS_DEV, slot_count, D), starts.reshape(batches, SEQS_DEV, slot_count), pick_list.reshape(batches, SEQS_DEV, slot_count), active.reshape(batches, SEQS_DEV, slot_count)))
        change = low_back(low(change.reshape(SEQS, slot_count, D)))
        update = gate_values[..., None] * change * active[..., None].astype(jnp.float32)
        residual = jax.vmap(lambda whole_seq, where_at, added_rows: whole_seq.at[where_at].add(added_rows))(residual, pick_list, update)
    return residual

def reference(tokens, attention_gain, query_weight, key_weight, value_weight, output_weight, feed_gain, gate_weight, up_weight, down_weight, router, out_grad, doc_lengths, picks_first, picks_second, picks_third, routes):
    lengths_flat = doc_lengths.reshape(SEQS, NDOC)
    doc_ends = jnp.cumsum(lengths_flat, axis=-1).astype(jnp.int32)
    routes_flat = routes.reshape(SEQS, NREC, 2)
    layouts = []
    for recursion, pick_table in enumerate((picks_first, picks_second, picks_third)):
        pick_list = pick_table.reshape(SEQS, -1).astype(jnp.int32)
        slot_count = pick_list.shape[1]
        active = jnp.arange(slot_count)[None, :] < routes_flat[:, recursion, 0][:, None]
        starts = lax.optimization_barrier(jnp.sum(jnp.where(doc_ends[:, None, :] <= pick_list[:, :, None], lengths_flat[:, None, :], 0), axis=-1)).astype(jnp.int32)
        layouts.append((pick_list, active, starts))
    floats = tuple((argument.astype(jnp.float32) for argument in (tokens, attention_gain, query_weight, key_weight, value_weight, output_weight, feed_gain, gate_weight, up_weight, down_weight, router)))

    def whole_block(*values):
        return forward(values[1:10], values[10], values[0], layouts)
    result, pullback = jax.vjp(whole_block, *floats)
    gradients = pullback(out_grad.astype(jnp.float32))
    return (result.astype(jnp.bfloat16), gradients[0].astype(jnp.bfloat16), gradients[1], gradients[2], gradients[3], gradients[4], gradients[5], gradients[6], gradients[7], gradients[8], gradients[9], gradients[10])
```

```python
import jax
import jax.numpy as jnp
from jax import lax
from jax.sharding import PartitionSpec as P

HEAD_DIM = 64
NREC = 3


EPSILON = 1e-05
ROPE_BASE = 10000.0
SCORE_SCALE = 0.125
MASKED = -1e30


def rms_scale(values):
    return lax.rsqrt(jnp.mean(values * values, axis=-1, keepdims=True) + EPSILON)


def exact_parts(values):
    upper = values.astype(jnp.bfloat16)
    rest = values - upper.astype(jnp.float32)
    middle_part = rest.astype(jnp.bfloat16)
    lowest = (rest - middle_part.astype(jnp.float32)).astype(jnp.bfloat16)
    return (upper, middle_part, lowest)


def pick_rows(whole, selector):
    parts = exact_parts(whole)
    taken = [
        jnp.einsum("sjp,spd->sjd", selector, piece, preferred_element_type=jnp.float32)
        for piece in parts
    ]
    return taken[0] + taken[1] + taken[2]


def place_rows(whole, selector, added):
    parts = exact_parts(added)
    spread = [
        jnp.einsum("sjp,sjd->spd", selector, piece, preferred_element_type=jnp.float32)
        for piece in parts
    ]
    return whole + (spread[0] + spread[1] + spread[2])


def rope_tables(positions):
    halfway = HEAD_DIM // 2
    inverse = ROPE_BASE ** (-(jnp.arange(halfway, dtype=jnp.float32) * (2.0 / HEAD_DIM)))
    angles = positions.astype(jnp.float32)[..., None] * inverse
    cosines = jnp.cos(angles)
    sine_values = jnp.sin(angles)
    return (
        jnp.concatenate([cosines, cosines], -1),
        jnp.concatenate([sine_values, sine_values], -1),
    )


def rotate(values, cosines, sine_values):
    halfway = values.shape[-1] // 2
    turned = jnp.concatenate([-values[..., halfway:], values[..., :halfway]], -1)
    return values * cosines + turned * sine_values


def unrotate(grads_in, cosines, sine_values):
    halfway = grads_in.shape[-1] // 2
    scaled = grads_in * sine_values
    return grads_in * cosines + jnp.concatenate([scaled[..., halfway:], -scaled[..., :halfway]], -1)


def attention_mask(labels, starts, positions, active):
    same_doc = (labels[:, :, None] == labels[:, None, :]) & (
        starts[:, :, None] == starts[:, None, :]
    )
    causal = positions[:, None, :] <= positions[:, :, None]
    length = labels.shape[1]
    return same_doc & causal & active[:, None, :] | jnp.eye(length, dtype=bool)[None]


def block_inner(rows_low, allowed, positions, weights, kept_lse):
    (
        attention_gain,
        query_weight,
        key_weight,
        value_weight,
        output_weight,
        feed_gain,
        gate_weight,
        up_weight,
        down_weight,
    ) = weights
    group_count, length, model_width = rows_low.shape
    kv_count = key_weight.shape[1] // HEAD_DIM
    per_group = query_weight.shape[1] // key_weight.shape[1]
    flat_rows = rows_low.reshape(group_count * length, model_width).astype(jnp.float32)
    inverse_one = rms_scale(flat_rows)
    normed_one = (flat_rows * inverse_one * attention_gain).astype(jnp.bfloat16)
    query_rows = jnp.dot(normed_one, query_weight, preferred_element_type=jnp.float32)
    key_pre = jnp.dot(normed_one, key_weight, preferred_element_type=jnp.float32)
    value_low = jnp.dot(normed_one, value_weight, preferred_element_type=jnp.float32).astype(
        jnp.bfloat16
    )
    cosines, sine_values = rope_tables(positions)
    query_low = rotate(
        query_rows.reshape(group_count, length, kv_count, per_group, HEAD_DIM),
        cosines[:, :, None, None],
        sine_values[:, :, None, None],
    ).astype(jnp.bfloat16)
    key_low = rotate(
        key_pre.reshape(group_count, length, kv_count, HEAD_DIM),
        cosines[:, :, None],
        sine_values[:, :, None],
    ).astype(jnp.bfloat16)
    value_low = value_low.reshape(group_count, length, kv_count, HEAD_DIM)
    scores = (
        jnp.einsum("gqkhd,gskd->gkhqs", query_low, key_low, preferred_element_type=jnp.float32)
        * SCORE_SCALE
    )
    scores = jnp.where(allowed[:, None, None], scores, MASKED)
    if kept_lse is None:
        highest = jnp.max(scores, axis=-1, keepdims=True)
        kept_lse = highest + jnp.log(jnp.sum(jnp.exp(scores - highest), axis=-1, keepdims=True))
    shares = jnp.exp(scores - kept_lse)
    shares_low = shares.astype(jnp.bfloat16)
    mixed_rows = jnp.einsum(
        "gkhqs,gskd->gqkhd", shares_low, value_low, preferred_element_type=jnp.float32
    )
    mixed_low = mixed_rows.reshape(group_count * length, model_width).astype(jnp.bfloat16)
    attended = jnp.dot(mixed_low, output_weight, preferred_element_type=jnp.float32)
    middle = flat_rows + attended
    inverse_two = rms_scale(middle)
    normed_two = (middle * inverse_two * feed_gain).astype(jnp.bfloat16)
    gate_pre = jnp.dot(normed_two, gate_weight, preferred_element_type=jnp.float32)
    up_pre = jnp.dot(normed_two, up_weight, preferred_element_type=jnp.float32)
    hidden = (jax.nn.silu(gate_pre) * up_pre).astype(jnp.bfloat16)
    return (
        flat_rows,
        inverse_one,
        normed_one,
        query_low,
        key_low,
        value_low,
        cosines,
        sine_values,
        shares,
        shares_low,
        mixed_low,
        attended,
        middle,
        inverse_two,
        normed_two,
        gate_pre,
        up_pre,
        hidden,
        kept_lse,
    )


def block_forward(rows_low, allowed, positions, weights):
    inner = block_inner(rows_low, allowed, positions, weights, None)
    attended = inner[11]
    hidden = inner[17]
    change = attended + jnp.dot(hidden, weights[8], preferred_element_type=jnp.float32)
    return (change, inner[18])


def block_backward(rows_low, allowed, positions, kept_lse, change_grad, weights):
    (
        attention_gain,
        query_weight,
        key_weight,
        value_weight,
        output_weight,
        feed_gain,
        gate_weight,
        up_weight,
        down_weight,
    ) = weights
    (
        flat_rows,
        inverse_one,
        normed_one,
        query_low,
        key_low,
        value_low,
        cosines,
        sine_values,
        shares,
        shares_low,
        mixed_low,
        attended,
        middle,
        inverse_two,
        normed_two,
        gate_pre,
        up_pre,
        hidden,
        kept_lse,
    ) = block_inner(rows_low, allowed, positions, weights, kept_lse)
    group_count, length, model_width = rows_low.shape
    kv_count = key_weight.shape[1] // HEAD_DIM
    per_group = query_weight.shape[1] // key_weight.shape[1]
    change_flat = change_grad.reshape(group_count * length, model_width)
    grad_down = jnp.einsum("rf,rd->fd", hidden, change_flat, preferred_element_type=jnp.float32)
    hidden_grad = jnp.einsum(
        "rd,fd->rf", change_flat, down_weight, preferred_element_type=jnp.float32
    )
    gate_sigmoid = jax.nn.sigmoid(gate_pre)
    gate_grad = (
        hidden_grad * up_pre * (gate_sigmoid + gate_pre * gate_sigmoid * (1.0 - gate_sigmoid))
    ).astype(jnp.bfloat16)
    up_grad = (hidden_grad * gate_pre * gate_sigmoid).astype(jnp.bfloat16)
    grad_gate = jnp.einsum("rd,rf->df", normed_two, gate_grad, preferred_element_type=jnp.float32)
    grad_up = jnp.einsum("rd,rf->df", normed_two, up_grad, preferred_element_type=jnp.float32)
    normed_two_grad = jnp.einsum(
        "rf,df->rd", gate_grad, gate_weight, preferred_element_type=jnp.float32
    ) + jnp.einsum("rf,df->rd", up_grad, up_weight, preferred_element_type=jnp.float32)
    scaled_two = middle * inverse_two
    grad_feed_gain = jnp.sum(normed_two_grad * scaled_two, axis=0)
    upstream_two = normed_two_grad * feed_gain
    middle_grad = inverse_two * (
        upstream_two - scaled_two * jnp.mean(upstream_two * scaled_two, axis=-1, keepdims=True)
    )
    attended_grad = (change_flat.astype(jnp.float32) + middle_grad).astype(jnp.bfloat16)
    grad_output = jnp.einsum(
        "rc,rd->cd", mixed_low, attended_grad, preferred_element_type=jnp.float32
    )
    mixed_grad = jnp.einsum(
        "rd,cd->rc", attended_grad, output_weight, preferred_element_type=jnp.float32
    ).astype(jnp.bfloat16)
    mixed_grad = mixed_grad.reshape(group_count, length, kv_count, per_group, HEAD_DIM)
    prob_grad = jnp.einsum(
        "gqkhd,gskd->gkhqs", mixed_grad, value_low, preferred_element_type=jnp.float32
    )
    value_sum = jnp.einsum(
        "gkhqs,gqkhd->gskd", shares_low, mixed_grad, preferred_element_type=jnp.float32
    )
    score_grad = (
        shares * (prob_grad - jnp.sum(shares * prob_grad, axis=-1, keepdims=True))
    ).astype(jnp.bfloat16)
    query_back = (
        jnp.einsum("gkhqs,gskd->gqkhd", score_grad, key_low, preferred_element_type=jnp.float32)
        * SCORE_SCALE
    )
    key_back = (
        jnp.einsum("gkhqs,gqkhd->gskd", score_grad, query_low, preferred_element_type=jnp.float32)
        * SCORE_SCALE
    )
    query_grad = (
        unrotate(query_back, cosines[:, :, None, None], sine_values[:, :, None, None])
        .astype(jnp.bfloat16)
        .reshape(group_count * length, model_width)
    )
    key_grad = (
        unrotate(key_back, cosines[:, :, None], sine_values[:, :, None])
        .astype(jnp.bfloat16)
        .reshape(group_count * length, kv_count * HEAD_DIM)
    )
    value_grad = value_sum.astype(jnp.bfloat16).reshape(group_count * length, kv_count * HEAD_DIM)
    grad_query = jnp.einsum("rd,rc->dc", normed_one, query_grad, preferred_element_type=jnp.float32)
    grad_key = jnp.einsum("rd,rc->dc", normed_one, key_grad, preferred_element_type=jnp.float32)
    grad_value = jnp.einsum("rd,rc->dc", normed_one, value_grad, preferred_element_type=jnp.float32)
    normed_one_grad = (
        jnp.einsum("rc,dc->rd", query_grad, query_weight, preferred_element_type=jnp.float32)
        + jnp.einsum("rc,dc->rd", key_grad, key_weight, preferred_element_type=jnp.float32)
        + jnp.einsum("rc,dc->rd", value_grad, value_weight, preferred_element_type=jnp.float32)
    )
    scaled_one = flat_rows * inverse_one
    grad_attention_gain = jnp.sum(normed_one_grad * scaled_one, axis=0)
    upstream_one = normed_one_grad * attention_gain
    rows_grad = middle_grad + inverse_one * (
        upstream_one - scaled_one * jnp.mean(upstream_one * scaled_one, axis=-1, keepdims=True)
    )
    return (
        rows_grad,
        (
            grad_attention_gain,
            grad_query,
            grad_key,
            grad_value,
            grad_output,
            grad_feed_gain,
            grad_gate,
            grad_up,
            grad_down,
        ),
    )


def per_device(
    tokens,
    attention_gain,
    query_weight,
    key_weight,
    value_weight,
    output_weight,
    feed_gain,
    gate_weight,
    up_weight,
    down_weight,
    router,
    out_grad,
    doc_lengths,
    picks_first,
    picks_second,
    picks_third,
    routes,
):
    seq_count, seq_len, model_width = tokens.shape
    own_bucket = lax.axis_index("grp")
    weights = (
        attention_gain.astype(jnp.float32),
        query_weight,
        key_weight,
        value_weight,
        output_weight,
        feed_gain.astype(jnp.float32),
        gate_weight,
        up_weight,
        down_weight,
    )
    router_rows = router.astype(jnp.float32)
    lengths = jnp.take(doc_lengths, own_bucket, axis=0)
    doc_ends = jnp.cumsum(lengths, axis=-1)
    counts = jnp.take(routes, own_bucket, axis=0)[:, :, 0]
    seq_positions = jnp.arange(seq_len, dtype=jnp.int32)
    picks = [jnp.take(t, own_bucket, axis=0) for t in (picks_first, picks_second, picks_third)]
    actives = [
        jnp.arange(p.shape[-1])[None, :] < counts[:, r][:, None] for r, p in enumerate(picks)
    ]
    selectors = []
    for r in range(NREC):
        outer = jnp.broadcast_to(seq_positions[None], (seq_count, seq_len)) if r == 0 else picks[r - 1]
        hit = (picks[r][:, :, None] == outer[:, None, :]) & actives[r][:, :, None]
        if r > 0:
            hit = hit & actives[r - 1][:, None, :]
        selectors.append(hit.astype(jnp.bfloat16))
    touched = jnp.any(selectors[0] > 0, axis=1)
    stored = []
    states = []
    rows_now = jnp.einsum("sjp,spd->sjd", selectors[0], tokens, preferred_element_type=jnp.float32)
    for r in range(NREC):
        picked_rows = rows_now
        active = actives[r]
        gate_values = jax.nn.sigmoid(jnp.sum(picked_rows * router_rows[r], axis=-1))
        rows_low = picked_rows.astype(jnp.bfloat16)
        starts = jnp.sum(
            jnp.where(doc_ends[:, None, :] <= picks[r][..., None], lengths[:, None, :], 0), axis=-1
        )
        allowed = attention_mask(jnp.zeros_like(picks[r]), starts, picks[r], active)
        change, log_total = block_forward(rows_low, allowed, picks[r], weights)
        change_rows = change.astype(jnp.bfloat16).astype(jnp.float32).reshape(picked_rows.shape)
        stored.append((picked_rows, gate_values, rows_low, allowed, change_rows, log_total))
        update = gate_values[..., None] * change_rows * active[..., None].astype(jnp.float32)
        states.append(picked_rows + update)
        if r + 1 < NREC:
            rows_now = pick_rows(states[r], selectors[r + 1])
    final = states[-1]
    for r in (1, 0):
        inside = jnp.any(selectors[r + 1] > 0, axis=1)
        parts = exact_parts(final)
        spread = sum(
            jnp.einsum("sjp,sjd->spd", selectors[r + 1], part, preferred_element_type=jnp.float32)
            for part in parts
        )
        final = jnp.where(inside[..., None], spread, states[r])
    placed = jnp.einsum(
        "sjp,sjd->spd", selectors[0], final.astype(jnp.bfloat16), preferred_element_type=jnp.float32
    ).astype(jnp.bfloat16)
    out_state = jnp.where(touched[..., None], placed, tokens)

    grads = [jnp.einsum("sjp,spd->sjd", selectors[0], out_grad, preferred_element_type=jnp.float32)]
    for r in (1, 2):
        grads.append(
            jnp.einsum(
                "sjp,spd->sjd",
                selectors[r],
                grads[-1].astype(jnp.bfloat16),
                preferred_element_type=jnp.float32,
            )
        )
    grad_totals = tuple((jnp.zeros(weight_item.shape, jnp.float32) for weight_item in weights))
    router_terms = [None] * NREC
    for r in (2, 1, 0):
        picked_rows, gate_values, rows_low, allowed, change_rows, log_total = stored[r]
        row_grad = grads[r]
        active_float = actives[r].astype(jnp.float32)
        change_grad = (gate_values[..., None] * row_grad * active_float[..., None]).astype(
            jnp.bfloat16
        )
        logit_grad = (
            jnp.sum(row_grad * change_rows, axis=-1)
            * active_float
            * gate_values
            * (1.0 - gate_values)
        )
        router_terms[r] = jnp.sum(logit_grad[..., None] * picked_rows, axis=(0, 1))
        rows_grad, grad_terms = block_backward(
            rows_low, allowed, picks[r], log_total, change_grad, weights
        )
        grad_totals = tuple(
            (running + fresh_term for running, fresh_term in zip(grad_totals, grad_terms))
        )
        sent_grad = rows_grad.astype(jnp.bfloat16).astype(jnp.float32).reshape(row_grad.shape)
        total = (logit_grad[..., None] * router_rows[r] + sent_grad) * active_float[..., None]
        grads[r] = row_grad + total
        extra = total if r == 2 else extra + total
        if r > 0:
            extra = place_rows(jnp.zeros_like(grads[r - 1]), selectors[r], extra)
            grads[r - 1] = grads[r - 1] + extra
    placed_grad = jnp.einsum(
        "sjp,sjd->spd", selectors[0], grads[0].astype(jnp.bfloat16), preferred_element_type=jnp.float32
    ).astype(jnp.bfloat16)
    grad_tokens = jnp.where(touched[..., None], placed_grad, out_grad)
    router_grad = jnp.stack(router_terms, 0)
    sums = lax.psum(grad_totals + (router_grad,), ("grp", "rep"))
    return (out_state, grad_tokens) + tuple(sums)


def solution(mesh):
    placed = (
        P(("grp", "rep"), None, None),
        P(),
        P(),
        P(),
        P(),
        P(),
        P(),
        P(),
        P(),
        P(),
        P(),
        P(("grp", "rep"), None, None),
        P(None, "rep", None),
        P(None, "rep", None),
        P(None, "rep", None),
        P(None, "rep", None),
        P(None, "rep", None, None),
    )
    return jax.shard_map(
        per_device,
        mesh=mesh,
        in_specs=placed,
        out_specs=(
            P(("grp", "rep"), None, None),
            P(("grp", "rep"), None, None),
            P(),
            P(),
            P(),
            P(),
            P(),
            P(),
            P(),
            P(),
            P(),
            P(),
        ),
        check_vma=False,
    )
```

```python
import functools

import jax
import jax.numpy as jnp
from jax import lax
from jax.experimental import pallas as pl
from jax.experimental.pallas import tpu as pltpu
from jax.sharding import PartitionSpec as P

HEAD_DIM = 64
NREC = 3


EPSILON = 1e-05
ROPE_BASE = 10000.0
SCORE_SCALE = 0.125
MASKED = -1e30


MESH = pl.DeviceIdType.MESH
ROWS = 576
LANES = 128

def grid_of(groups, replicas):
    cores = 2 if groups % 2 == 0 else 1
    fast = 2 if replicas == 8 else (4 if replicas % 4 == 0 else 1)
    return cores, groups // cores, fast, replicas // fast


class Ring:
    def __init__(self, groups, replicas):
        self.cores, self.nx, self.ny, self.nz = grid_of(groups, replicas)
        self.sizes = {"c": self.cores, "x": self.nx, "y": self.ny, "z": self.nz}
        g, r = lax.axis_index("grp"), lax.axis_index("rep")
        self.at = {"c": g % self.cores, "x": g // self.cores, "y": r % self.ny, "z": r // self.ny}

    def peer(self, axis, step):
        at = dict(self.at)
        at[axis] = lax.rem(at[axis] + step, self.sizes[axis])
        return (at["x"] * self.cores + at["c"], at["z"] * self.ny + at["y"])

    def index(self, axis, step):
        return lax.rem(self.at[axis] + step, self.sizes[axis])


def add_blocks(dst, dst_at, srcs, count, rows):
    def body(i, c):
        total = None
        for ref, at in srcs:
            v = ref[at + i].astype(jnp.float32)
            total = v if total is None else total + v
        dst[dst_at + i] = total.astype(dst.dtype)
        return c
    lax.fori_loop(0, count, body, 0)


class Exchange:
    def __init__(self, ring, own, full, rc, r1, r2, r3, send, recv, units):
        self.__dict__.update(locals())
        self.tail = []
        n = ring.sizes
        self.lead = n["c"] * n["x"] * n["y"]

    def order(self, u):
        return ("x", "y") if u % 2 == 0 else ("y", "x")

    def copy(self, u, phase, step, src, dst, axis):
        k = step - 1
        cp = pltpu.make_async_remote_copy(
            src_ref=src, dst_ref=dst,
            send_sem=self.send.at[u, phase, k], recv_sem=self.recv.at[u, phase, k],
            device_id=self.ring.peer(axis, step), device_id_type=MESH)
        cp.start()
        self.tail.append(cp)
        return cp

    def base(self, u):
        return u * self.lead

    def start(self, u, s):
        ring, n = self.ring, self.ring.sizes
        a1, a2 = self.order(u)
        n1, n2, nz = n[a1], n[a2], n["z"]
        half = n1 * n2
        b = self.base(u)
        mc, m1, m2, mz = ring.at["c"], ring.at[a1], ring.at[a2], ring.at["z"]
        rows = ROWS // nz
        mine = b + mc * half
        piece1 = mine + m1 * n2
        piece2 = piece1 + m2
        zrows = pl.ds(pl.multiple_of(mz * rows, 16), rows)
        own, full = self.own, self.full
        if s == 0:
            for k in range(1, n["c"]):
                to = b + ring.index("c", k) * half
                self.copy(u, 0, k, own.at[pl.ds(to, half)], self.rc.at[u], "c")
        elif s == 1:
            self.wait(u, 0, n["c"])
            if n["c"] > 1:
                add_blocks(own, mine, [(own, mine), (self.rc.at[u], 0)], half, ROWS)
            for k in range(1, n1):
                to = mine + ring.index(a1, k) * n2
                self.copy(u, 1, k, own.at[pl.ds(to, n2)], self.r1.at[u, k - 1, pl.ds(0, n2)], a1)
        elif s == 2:
            self.wait(u, 1, n1)
            if n1 > 1:
                add_blocks(own, piece1, [(own, piece1)] + [(self.r1.at[u, k - 1], 0) for k in range(1, n1)], n2, ROWS)
            for k in range(1, n2):
                to = piece1 + ring.index(a2, k)
                self.copy(u, 2, k, own.at[to], self.r2.at[u, k - 1], a2)
        elif s == 3:
            self.wait(u, 2, n2)
            if n2 > 1:
                total = own[piece2].astype(jnp.float32)
                for k in range(1, n2):
                    total = total + self.r2[u, k - 1].astype(jnp.float32)
                own[piece2] = total.astype(own.dtype)
            for k in range(1, nz):
                to = pl.ds(pl.multiple_of(ring.index("z", k) * rows, 16), rows)
                self.copy(u, 3, k, own.at[piece2, to], self.r3.at[u, k - 1], "z")
        elif s == 4:
            self.wait(u, 3, nz)
            total = own[piece2, zrows].astype(jnp.float32)
            for k in range(1, nz):
                total = total + self.r3[u, k - 1].astype(jnp.float32)
            full[piece2, zrows] = total.astype(own.dtype)
            for k in range(1, nz):
                self.copy(u, 4, k, full.at[piece2, zrows], full.at[piece2, zrows], "z")
        elif s == 5:
            self.wait(u, 4, nz)
            for k in range(1, n2):
                self.copy(u, 5, k, full.at[piece2], full.at[piece2], a2)
        elif s == 6:
            self.wait(u, 5, n2)
            for k in range(1, n1):
                self.copy(u, 6, k, full.at[pl.ds(piece1, n2)], full.at[pl.ds(piece1, n2)], a1)
        elif s == 7:
            self.wait(u, 6, n1)
            for k in range(1, n["c"]):
                self.copy(u, 7, k, full.at[pl.ds(mine, half)], full.at[pl.ds(mine, half)], "c")
        elif s == 8:
            self.wait(u, 7, n["c"])

    def wait(self, u, phase, size):
        for cp in self.pending.pop((u, phase), []):
            cp.wait_recv()

    pending = None


def make_exchange(*a):
    e = Exchange(*a)
    e.pending = {}
    orig = e.copy
    def copy(u, phase, step, src, dst, axis):
        cp = orig(u, phase, step, src, dst, axis)
        e.pending.setdefault((u, phase), []).append(cp)
        return cp
    e.copy = copy
    return e


def barrier(ring):
    sem = pltpu.get_barrier_semaphore()
    count = 0
    for axis, size in ring.sizes.items():
        for k in range(1, size):
            pl.semaphore_signal(sem, inc=1, device_id=ring.peer(axis, k), device_id_type=MESH)
            count += 1
    pl.semaphore_wait(sem, count)


def reduce_kernel(groups, replicas, units, lag, own_in, small_in, full, small_out, own, rc, r1, r2, r3, sm, send, recv, ssend, srecv):
    ring = Ring(groups, replicas)
    barrier(ring)
    ex = make_exchange(ring, own, full, rc, r1, r2, r3, send, recv, units)
    smalls = []
    axes = ["c", "x", "y", "z"]
    def small_send(p):
        ax = axes[p]
        n = ring.sizes[ax]
        src = sm.at[p, ring.at[ax]]
        cps = []
        for k in range(1, n):
            cp = pltpu.make_async_remote_copy(src_ref=src, dst_ref=src, send_sem=ssend.at[p, k - 1], recv_sem=srecv.at[p, k - 1],
                                              device_id=ring.peer(ax, k), device_id_type=MESH)
            cp.start(); cps.append(cp)
        smalls.append(cps)
    def small_add(p):
        ax = axes[p]
        for cp in smalls[p]:
            cp.wait_recv()
        total = sm[p, 0]
        for j in range(1, ring.sizes[ax]):
            total = total + sm[p, j]
        return total
    own[...] = own_in[...]
    sm[0, ring.at["c"]] = small_in[...]
    small_send(0)
    steps = 9
    for t in range(steps + lag * ((units - 1) // 2) ):
        for u in range(units):
            s = t - lag * (u // 2)
            if 0 <= s < steps:
                ex.start(u, s)
        if t < 3:
            v = small_add(t)
            sm[t + 1, ring.at[axes[t + 1]]] = v
            small_send(t + 1)
        elif t == 3:
            small_out[...] = small_add(3)
    for cps in smalls:
        for cp in cps:
            cp.wait_send()
    for cp in ex.tail:
        cp.wait_send()


def all_reduce(own, small, groups, replicas, lag=1):
    cores, nx, ny, nz = grid_of(groups, replicas)
    lead = cores * nx * ny
    units = own.shape[0] // lead
    nm = max(nx, ny)
    peers = max(cores, nx, ny, nz) - 1
    scratch = [
        pltpu.VMEM(own.shape, own.dtype),
        pltpu.VMEM((units, lead // cores, ROWS, LANES), own.dtype),
        pltpu.VMEM((units, nm - 1, nm, ROWS, LANES), own.dtype),
        pltpu.VMEM((units, nm - 1, ROWS, LANES), own.dtype),
        pltpu.VMEM((units, nz - 1, ROWS // nz, LANES), own.dtype),
        pltpu.VMEM((4, max(cores, nx, ny, nz)) + small.shape, jnp.float32),
        pltpu.SemaphoreType.DMA((units, 8, peers)),
        pltpu.SemaphoreType.DMA((units, 8, peers)),
        pltpu.SemaphoreType.DMA((4, peers)),
        pltpu.SemaphoreType.DMA((4, peers)),
    ]
    vm = pl.BlockSpec(memory_space=pltpu.VMEM)
    return pl.pallas_call(
        functools.partial(reduce_kernel, groups, replicas, units, lag),
        out_shape=(jax.ShapeDtypeStruct(own.shape, own.dtype), jax.ShapeDtypeStruct(small.shape, small.dtype)),
        in_specs=[vm, vm], out_specs=(vm, vm), scratch_shapes=scratch,
        compiler_params=pltpu.CompilerParams(collective_id=0, has_side_effects=True, vmem_limit_bytes=60 * 2**20),
        name="grad_sum",
    )(own, small)


def lanes_first(table):
    rows, columns = table.shape
    return table.reshape(rows, columns // LANES, LANES).transpose(1, 0, 2)


def lanes_last(blocks):
    count, rows, width = blocks.shape
    return blocks.transpose(1, 0, 2).reshape(rows, count * width)


def sum_gradients(grads, router_grad):
    gain_one, query, key, value, output, gain_two, gate, up, down = grads
    groups, replicas = lax.axis_size("grp"), lax.axis_size("rep")
    if groups * replicas == 1:
        return grads + (router_grad,)
    cores, nx, ny, nz = grid_of(groups, replicas)
    packed = jnp.concatenate(
        [
            lanes_first(part.astype(jnp.bfloat16))
            for part in (
                down.T,
                gate,
                up,
                jnp.concatenate([query, key], 1),
                jnp.concatenate([value, output], 1),
            )
        ],
        0,
    )
    count = packed.shape[0]
    pad = -count % (cores * nx * ny)
    packed = jnp.pad(packed, ((0, pad), (0, 0), (0, 0)))
    small = jnp.concatenate([gain_one[None], gain_two[None], router_grad], 0)
    small = jnp.pad(small, ((0, 3), (0, -small.shape[1] % LANES)))
    full, sums = all_reduce(packed, small, groups, replicas)
    full = full.astype(jnp.float32)
    wide = gate.shape[1] // LANES
    narrow = (query.shape[1] + key.shape[1]) // LANES
    at = [0, wide, 2 * wide, 3 * wide, 3 * wide + narrow, 3 * wide + 2 * narrow]
    parts = [lanes_last(full[a:b]) for a, b in zip(at[:-1], at[1:])]
    width = query.shape[0]
    sums = sums[:5, :width]
    return (
        sums[0],
        parts[3][:, : query.shape[1]],
        parts[3][:, query.shape[1] :],
        parts[4][:, : value.shape[1]],
        parts[4][:, value.shape[1] :],
        sums[1],
        parts[1],
        parts[2],
        parts[0].T,
        sums[2:5],
    )


def rms_scale(values):
    return lax.rsqrt(jnp.mean(values * values, axis=-1, keepdims=True) + EPSILON)


def exact_parts(values):
    upper = values.astype(jnp.bfloat16)
    rest = values - upper.astype(jnp.float32)
    middle_part = rest.astype(jnp.bfloat16)
    lowest = (rest - middle_part.astype(jnp.float32)).astype(jnp.bfloat16)
    return (upper, middle_part, lowest)


def pick_rows(whole, selector):
    parts = exact_parts(whole)
    taken = [
        jnp.einsum("sjp,spd->sjd", selector, piece, preferred_element_type=jnp.float32)
        for piece in parts
    ]
    return taken[0] + taken[1] + taken[2]


def place_rows(whole, selector, added):
    parts = exact_parts(added)
    spread = [
        jnp.einsum("sjp,sjd->spd", selector, piece, preferred_element_type=jnp.float32)
        for piece in parts
    ]
    return whole + (spread[0] + spread[1] + spread[2])


def rope_tables(positions):
    halfway = HEAD_DIM // 2
    inverse = ROPE_BASE ** (-(jnp.arange(halfway, dtype=jnp.float32) * (2.0 / HEAD_DIM)))
    angles = positions.astype(jnp.float32)[..., None] * inverse
    cosines = jnp.cos(angles)
    sine_values = jnp.sin(angles)
    return (
        jnp.concatenate([cosines, cosines], -1),
        jnp.concatenate([sine_values, sine_values], -1),
    )


def rotate(values, cosines, sine_values):
    halfway = values.shape[-1] // 2
    turned = jnp.concatenate([-values[..., halfway:], values[..., :halfway]], -1)
    return values * cosines + turned * sine_values


def unrotate(grads_in, cosines, sine_values):
    halfway = grads_in.shape[-1] // 2
    scaled = grads_in * sine_values
    return grads_in * cosines + jnp.concatenate([scaled[..., halfway:], -scaled[..., :halfway]], -1)


def attention_mask(labels, starts, positions, active):
    same_doc = (labels[:, :, None] == labels[:, None, :]) & (
        starts[:, :, None] == starts[:, None, :]
    )
    causal = positions[:, None, :] <= positions[:, :, None]
    length = labels.shape[1]
    return same_doc & causal & active[:, None, :] | jnp.eye(length, dtype=bool)[None]


def block_inner(rows_low, allowed, positions, weights, kept_lse):
    (
        attention_gain,
        query_weight,
        key_weight,
        value_weight,
        output_weight,
        feed_gain,
        gate_weight,
        up_weight,
        down_weight,
    ) = weights
    group_count, length, model_width = rows_low.shape
    kv_count = key_weight.shape[1] // HEAD_DIM
    per_group = query_weight.shape[1] // key_weight.shape[1]
    flat_rows = rows_low.reshape(group_count * length, model_width).astype(jnp.float32)
    inverse_one = rms_scale(flat_rows)
    normed_one = (flat_rows * inverse_one * attention_gain).astype(jnp.bfloat16)
    query_rows = jnp.dot(normed_one, query_weight, preferred_element_type=jnp.float32)
    key_pre = jnp.dot(normed_one, key_weight, preferred_element_type=jnp.float32)
    value_low = jnp.dot(normed_one, value_weight, preferred_element_type=jnp.float32).astype(
        jnp.bfloat16
    )
    cosines, sine_values = rope_tables(positions)
    query_low = rotate(
        query_rows.reshape(group_count, length, kv_count, per_group, HEAD_DIM),
        cosines[:, :, None, None],
        sine_values[:, :, None, None],
    ).astype(jnp.bfloat16)
    key_low = rotate(
        key_pre.reshape(group_count, length, kv_count, HEAD_DIM),
        cosines[:, :, None],
        sine_values[:, :, None],
    ).astype(jnp.bfloat16)
    value_low = value_low.reshape(group_count, length, kv_count, HEAD_DIM)
    scores = (
        jnp.einsum("gqkhd,gskd->gkhqs", query_low, key_low, preferred_element_type=jnp.float32)
        * SCORE_SCALE
    )
    scores = jnp.where(allowed[:, None, None], scores, MASKED)
    if kept_lse is None:
        highest = jnp.max(scores, axis=-1, keepdims=True)
        kept_lse = highest + jnp.log(jnp.sum(jnp.exp(scores - highest), axis=-1, keepdims=True))
    shares = jnp.exp(scores - kept_lse)
    shares_low = shares.astype(jnp.bfloat16)
    mixed_rows = jnp.einsum(
        "gkhqs,gskd->gqkhd", shares_low, value_low, preferred_element_type=jnp.float32
    )
    mixed_low = mixed_rows.reshape(group_count * length, model_width).astype(jnp.bfloat16)
    attended = jnp.dot(mixed_low, output_weight, preferred_element_type=jnp.float32)
    middle = flat_rows + attended
    inverse_two = rms_scale(middle)
    normed_two = (middle * inverse_two * feed_gain).astype(jnp.bfloat16)
    gate_pre = jnp.dot(normed_two, gate_weight, preferred_element_type=jnp.float32)
    up_pre = jnp.dot(normed_two, up_weight, preferred_element_type=jnp.float32)
    hidden = (jax.nn.silu(gate_pre) * up_pre).astype(jnp.bfloat16)
    return (
        flat_rows,
        inverse_one,
        normed_one,
        query_low,
        key_low,
        value_low,
        cosines,
        sine_values,
        shares,
        shares_low,
        mixed_low,
        attended,
        middle,
        inverse_two,
        normed_two,
        gate_pre,
        up_pre,
        hidden,
        kept_lse,
    )


def block_forward(rows_low, allowed, positions, weights):
    inner = block_inner(rows_low, allowed, positions, weights, None)
    attended = inner[11]
    hidden = inner[17]
    change = attended + jnp.dot(hidden, weights[8], preferred_element_type=jnp.float32)
    return (change, inner[18])


def block_backward(rows_low, allowed, positions, kept_lse, change_grad, weights):
    (
        attention_gain,
        query_weight,
        key_weight,
        value_weight,
        output_weight,
        feed_gain,
        gate_weight,
        up_weight,
        down_weight,
    ) = weights
    (
        flat_rows,
        inverse_one,
        normed_one,
        query_low,
        key_low,
        value_low,
        cosines,
        sine_values,
        shares,
        shares_low,
        mixed_low,
        attended,
        middle,
        inverse_two,
        normed_two,
        gate_pre,
        up_pre,
        hidden,
        kept_lse,
    ) = block_inner(rows_low, allowed, positions, weights, kept_lse)
    group_count, length, model_width = rows_low.shape
    kv_count = key_weight.shape[1] // HEAD_DIM
    per_group = query_weight.shape[1] // key_weight.shape[1]
    change_flat = change_grad.reshape(group_count * length, model_width)
    grad_down = jnp.einsum("rf,rd->fd", hidden, change_flat, preferred_element_type=jnp.float32)
    hidden_grad = jnp.einsum(
        "rd,fd->rf", change_flat, down_weight, preferred_element_type=jnp.float32
    )
    gate_sigmoid = jax.nn.sigmoid(gate_pre)
    gate_grad = (
        hidden_grad * up_pre * (gate_sigmoid + gate_pre * gate_sigmoid * (1.0 - gate_sigmoid))
    ).astype(jnp.bfloat16)
    up_grad = (hidden_grad * gate_pre * gate_sigmoid).astype(jnp.bfloat16)
    grad_gate = jnp.einsum("rd,rf->df", normed_two, gate_grad, preferred_element_type=jnp.float32)
    grad_up = jnp.einsum("rd,rf->df", normed_two, up_grad, preferred_element_type=jnp.float32)
    normed_two_grad = jnp.einsum(
        "rf,df->rd", gate_grad, gate_weight, preferred_element_type=jnp.float32
    ) + jnp.einsum("rf,df->rd", up_grad, up_weight, preferred_element_type=jnp.float32)
    scaled_two = middle * inverse_two
    grad_feed_gain = jnp.sum(normed_two_grad * scaled_two, axis=0)
    upstream_two = normed_two_grad * feed_gain
    middle_grad = inverse_two * (
        upstream_two - scaled_two * jnp.mean(upstream_two * scaled_two, axis=-1, keepdims=True)
    )
    attended_grad = (change_flat.astype(jnp.float32) + middle_grad).astype(jnp.bfloat16)
    grad_output = jnp.einsum(
        "rc,rd->cd", mixed_low, attended_grad, preferred_element_type=jnp.float32
    )
    mixed_grad = jnp.einsum(
        "rd,cd->rc", attended_grad, output_weight, preferred_element_type=jnp.float32
    ).astype(jnp.bfloat16)
    mixed_grad = mixed_grad.reshape(group_count, length, kv_count, per_group, HEAD_DIM)
    prob_grad = jnp.einsum(
        "gqkhd,gskd->gkhqs", mixed_grad, value_low, preferred_element_type=jnp.float32
    )
    value_sum = jnp.einsum(
        "gkhqs,gqkhd->gskd", shares_low, mixed_grad, preferred_element_type=jnp.float32
    )
    score_grad = (
        shares * (prob_grad - jnp.sum(shares * prob_grad, axis=-1, keepdims=True))
    ).astype(jnp.bfloat16)
    query_back = (
        jnp.einsum("gkhqs,gskd->gqkhd", score_grad, key_low, preferred_element_type=jnp.float32)
        * SCORE_SCALE
    )
    key_back = (
        jnp.einsum("gkhqs,gqkhd->gskd", score_grad, query_low, preferred_element_type=jnp.float32)
        * SCORE_SCALE
    )
    query_grad = (
        unrotate(query_back, cosines[:, :, None, None], sine_values[:, :, None, None])
        .astype(jnp.bfloat16)
        .reshape(group_count * length, model_width)
    )
    key_grad = (
        unrotate(key_back, cosines[:, :, None], sine_values[:, :, None])
        .astype(jnp.bfloat16)
        .reshape(group_count * length, kv_count * HEAD_DIM)
    )
    value_grad = value_sum.astype(jnp.bfloat16).reshape(group_count * length, kv_count * HEAD_DIM)
    grad_query = jnp.einsum("rd,rc->dc", normed_one, query_grad, preferred_element_type=jnp.float32)
    grad_key = jnp.einsum("rd,rc->dc", normed_one, key_grad, preferred_element_type=jnp.float32)
    grad_value = jnp.einsum("rd,rc->dc", normed_one, value_grad, preferred_element_type=jnp.float32)
    normed_one_grad = (
        jnp.einsum("rc,dc->rd", query_grad, query_weight, preferred_element_type=jnp.float32)
        + jnp.einsum("rc,dc->rd", key_grad, key_weight, preferred_element_type=jnp.float32)
        + jnp.einsum("rc,dc->rd", value_grad, value_weight, preferred_element_type=jnp.float32)
    )
    scaled_one = flat_rows * inverse_one
    grad_attention_gain = jnp.sum(normed_one_grad * scaled_one, axis=0)
    upstream_one = normed_one_grad * attention_gain
    rows_grad = middle_grad + inverse_one * (
        upstream_one - scaled_one * jnp.mean(upstream_one * scaled_one, axis=-1, keepdims=True)
    )
    return (
        rows_grad,
        (
            grad_attention_gain,
            grad_query,
            grad_key,
            grad_value,
            grad_output,
            grad_feed_gain,
            grad_gate,
            grad_up,
            grad_down,
        ),
    )


def per_device(
    tokens,
    attention_gain,
    query_weight,
    key_weight,
    value_weight,
    output_weight,
    feed_gain,
    gate_weight,
    up_weight,
    down_weight,
    router,
    out_grad,
    doc_lengths,
    picks_first,
    picks_second,
    picks_third,
    routes,
):
    seq_count, seq_len, model_width = tokens.shape
    own_bucket = lax.axis_index("grp")
    weights = (
        attention_gain.astype(jnp.float32),
        query_weight,
        key_weight,
        value_weight,
        output_weight,
        feed_gain.astype(jnp.float32),
        gate_weight,
        up_weight,
        down_weight,
    )
    router_rows = router.astype(jnp.float32)
    lengths = jnp.take(doc_lengths, own_bucket, axis=0)
    doc_ends = jnp.cumsum(lengths, axis=-1)
    counts = jnp.take(routes, own_bucket, axis=0)[:, :, 0]
    seq_positions = jnp.arange(seq_len, dtype=jnp.int32)
    picks = [jnp.take(t, own_bucket, axis=0) for t in (picks_first, picks_second, picks_third)]
    actives = [
        jnp.arange(p.shape[-1])[None, :] < counts[:, r][:, None] for r, p in enumerate(picks)
    ]
    selectors = []
    for r in range(NREC):
        outer = jnp.broadcast_to(seq_positions[None], (seq_count, seq_len)) if r == 0 else picks[r - 1]
        hit = (picks[r][:, :, None] == outer[:, None, :]) & actives[r][:, :, None]
        if r > 0:
            hit = hit & actives[r - 1][:, None, :]
        selectors.append(hit.astype(jnp.bfloat16))
    touched = jnp.any(selectors[0] > 0, axis=1)
    stored = []
    states = []
    rows_now = jnp.einsum("sjp,spd->sjd", selectors[0], tokens, preferred_element_type=jnp.float32)
    for r in range(NREC):
        picked_rows = rows_now
        active = actives[r]
        gate_values = jax.nn.sigmoid(jnp.sum(picked_rows * router_rows[r], axis=-1))
        rows_low = picked_rows.astype(jnp.bfloat16)
        starts = jnp.sum(
            jnp.where(doc_ends[:, None, :] <= picks[r][..., None], lengths[:, None, :], 0), axis=-1
        )
        allowed = attention_mask(jnp.zeros_like(picks[r]), starts, picks[r], active)
        change, log_total = block_forward(rows_low, allowed, picks[r], weights)
        change_rows = change.astype(jnp.bfloat16).astype(jnp.float32).reshape(picked_rows.shape)
        stored.append((picked_rows, gate_values, rows_low, allowed, change_rows, log_total))
        update = gate_values[..., None] * change_rows * active[..., None].astype(jnp.float32)
        states.append(picked_rows + update)
        if r + 1 < NREC:
            rows_now = pick_rows(states[r], selectors[r + 1])
    final = states[-1]
    for r in (1, 0):
        inside = jnp.any(selectors[r + 1] > 0, axis=1)
        parts = exact_parts(final)
        spread = sum(
            jnp.einsum("sjp,sjd->spd", selectors[r + 1], part, preferred_element_type=jnp.float32)
            for part in parts
        )
        final = jnp.where(inside[..., None], spread, states[r])
    placed = jnp.einsum(
        "sjp,sjd->spd", selectors[0], final.astype(jnp.bfloat16), preferred_element_type=jnp.float32
    ).astype(jnp.bfloat16)
    out_state = jnp.where(touched[..., None], placed, tokens)

    grads = [jnp.einsum("sjp,spd->sjd", selectors[0], out_grad, preferred_element_type=jnp.float32)]
    for r in (1, 2):
        grads.append(
            jnp.einsum(
                "sjp,spd->sjd",
                selectors[r],
                grads[-1].astype(jnp.bfloat16),
                preferred_element_type=jnp.float32,
            )
        )
    grad_totals = tuple((jnp.zeros(weight_item.shape, jnp.float32) for weight_item in weights))
    router_terms = [None] * NREC
    for r in (2, 1, 0):
        picked_rows, gate_values, rows_low, allowed, change_rows, log_total = stored[r]
        row_grad = grads[r]
        active_float = actives[r].astype(jnp.float32)
        change_grad = (gate_values[..., None] * row_grad * active_float[..., None]).astype(
            jnp.bfloat16
        )
        logit_grad = (
            jnp.sum(row_grad * change_rows, axis=-1)
            * active_float
            * gate_values
            * (1.0 - gate_values)
        )
        router_terms[r] = jnp.sum(logit_grad[..., None] * picked_rows, axis=(0, 1))
        rows_grad, grad_terms = block_backward(
            rows_low, allowed, picks[r], log_total, change_grad, weights
        )
        grad_totals = tuple(
            (running + fresh_term for running, fresh_term in zip(grad_totals, grad_terms))
        )
        sent_grad = rows_grad.astype(jnp.bfloat16).astype(jnp.float32).reshape(row_grad.shape)
        total = (logit_grad[..., None] * router_rows[r] + sent_grad) * active_float[..., None]
        grads[r] = row_grad + total
        extra = total if r == 2 else extra + total
        if r > 0:
            extra = place_rows(jnp.zeros_like(grads[r - 1]), selectors[r], extra)
            grads[r - 1] = grads[r - 1] + extra
    placed_grad = jnp.einsum(
        "sjp,sjd->spd", selectors[0], grads[0].astype(jnp.bfloat16), preferred_element_type=jnp.float32
    ).astype(jnp.bfloat16)
    grad_tokens = jnp.where(touched[..., None], placed_grad, out_grad)
    router_grad = jnp.stack(router_terms, 0)
    sums = sum_gradients(grad_totals, router_grad)
    return (out_state, grad_tokens) + tuple(sums)


def solution(mesh):
    placed = (
        P(("grp", "rep"), None, None),
        P(),
        P(),
        P(),
        P(),
        P(),
        P(),
        P(),
        P(),
        P(),
        P(),
        P(("grp", "rep"), None, None),
        P(None, "rep", None),
        P(None, "rep", None),
        P(None, "rep", None),
        P(None, "rep", None),
        P(None, "rep", None, None),
    )
    return jax.shard_map(
        per_device,
        mesh=mesh,
        in_specs=placed,
        out_specs=(
            P(("grp", "rep"), None, None),
            P(("grp", "rep"), None, None),
            P(),
            P(),
            P(),
            P(),
            P(),
            P(),
            P(),
            P(),
            P(),
            P(),
        ),
        check_vma=False,
    )
```

```python
import functools
import math

import jax
import jax.numpy as jnp
import numpy as np
from jax import lax
from jax.experimental import pallas as pl
from jax.experimental.pallas import tpu as pltpu
from jax.sharding import PartitionSpec as P

HEAD_DIM = 64
NREC = 3


EPSILON = 1e-05
ROPE_BASE = 10000.0
SCORE_SCALE = 0.125
MASKED = -1e30


MESH = pl.DeviceIdType.MESH
ROWS = 576
LANES = 128

def grid_of(groups, replicas):
    cores = 2 if groups % 2 == 0 else 1
    fast = 2 if replicas == 8 else (4 if replicas % 4 == 0 else 1)
    return cores, groups // cores, fast, replicas // fast


class Ring:
    def __init__(self, groups, replicas):
        self.cores, self.nx, self.ny, self.nz = grid_of(groups, replicas)
        self.sizes = {"c": self.cores, "x": self.nx, "y": self.ny, "z": self.nz}
        g, r = lax.axis_index("grp"), lax.axis_index("rep")
        self.at = {"c": g % self.cores, "x": g // self.cores, "y": r % self.ny, "z": r // self.ny}

    def peer(self, axis, step):
        at = dict(self.at)
        at[axis] = lax.rem(at[axis] + step, self.sizes[axis])
        return (at["x"] * self.cores + at["c"], at["z"] * self.ny + at["y"])

    def index(self, axis, step):
        return lax.rem(self.at[axis] + step, self.sizes[axis])


def add_blocks(dst, dst_at, srcs, count, rows):
    def body(i, c):
        total = None
        for ref, at in srcs:
            v = ref[at + i].astype(jnp.float32)
            total = v if total is None else total + v
        dst[dst_at + i] = total.astype(dst.dtype)
        return c
    lax.fori_loop(0, count, body, 0)


class Exchange:
    def __init__(self, ring, own, full, rc, r1, r2, r3, send, recv, units):
        self.__dict__.update(locals())
        self.tail = []
        n = ring.sizes
        self.lead = n["c"] * n["x"] * n["y"]

    def order(self, u):
        return ("x", "y") if u % 2 == 0 else ("y", "x")

    def copy(self, u, phase, step, src, dst, axis):
        k = step - 1
        cp = pltpu.make_async_remote_copy(
            src_ref=src, dst_ref=dst,
            send_sem=self.send.at[u, phase, k], recv_sem=self.recv.at[u, phase, k],
            device_id=self.ring.peer(axis, step), device_id_type=MESH)
        cp.start()
        self.tail.append(cp)
        return cp

    def base(self, u):
        return u * self.lead

    def start(self, u, s):
        ring, n = self.ring, self.ring.sizes
        a1, a2 = self.order(u)
        n1, n2, nz = n[a1], n[a2], n["z"]
        half = n1 * n2
        b = self.base(u)
        mc, m1, m2, mz = ring.at["c"], ring.at[a1], ring.at[a2], ring.at["z"]
        rows = ROWS // nz
        mine = b + mc * half
        piece1 = mine + m1 * n2
        piece2 = piece1 + m2
        zrows = pl.ds(pl.multiple_of(mz * rows, 16), rows)
        own, full = self.own, self.full
        if s == 0:
            for k in range(1, n["c"]):
                to = b + ring.index("c", k) * half
                self.copy(u, 0, k, own.at[pl.ds(to, half)], self.rc.at[u], "c")
        elif s == 1:
            self.wait(u, 0, n["c"])
            if n["c"] > 1:
                add_blocks(own, mine, [(own, mine), (self.rc.at[u], 0)], half, ROWS)
            for k in range(1, n1):
                to = mine + ring.index(a1, k) * n2
                self.copy(u, 1, k, own.at[pl.ds(to, n2)], self.r1.at[u, k - 1, pl.ds(0, n2)], a1)
        elif s == 2:
            self.wait(u, 1, n1)
            if n1 > 1:
                add_blocks(own, piece1, [(own, piece1)] + [(self.r1.at[u, k - 1], 0) for k in range(1, n1)], n2, ROWS)
            for k in range(1, n2):
                to = piece1 + ring.index(a2, k)
                self.copy(u, 2, k, own.at[to], self.r2.at[u, k - 1], a2)
        elif s == 3:
            self.wait(u, 2, n2)
            if n2 > 1:
                total = own[piece2].astype(jnp.float32)
                for k in range(1, n2):
                    total = total + self.r2[u, k - 1].astype(jnp.float32)
                own[piece2] = total.astype(own.dtype)
            for k in range(1, nz):
                to = pl.ds(pl.multiple_of(ring.index("z", k) * rows, 16), rows)
                self.copy(u, 3, k, own.at[piece2, to], self.r3.at[u, k - 1], "z")
        elif s == 4:
            self.wait(u, 3, nz)
            total = own[piece2, zrows].astype(jnp.float32)
            for k in range(1, nz):
                total = total + self.r3[u, k - 1].astype(jnp.float32)
            full[piece2, zrows] = total.astype(own.dtype)
            for k in range(1, nz):
                self.copy(u, 4, k, full.at[piece2, zrows], full.at[piece2, zrows], "z")
        elif s == 5:
            self.wait(u, 4, nz)
            for k in range(1, n2):
                self.copy(u, 5, k, full.at[piece2], full.at[piece2], a2)
        elif s == 6:
            self.wait(u, 5, n2)
            for k in range(1, n1):
                self.copy(u, 6, k, full.at[pl.ds(piece1, n2)], full.at[pl.ds(piece1, n2)], a1)
        elif s == 7:
            self.wait(u, 6, n1)
            for k in range(1, n["c"]):
                self.copy(u, 7, k, full.at[pl.ds(mine, half)], full.at[pl.ds(mine, half)], "c")
        elif s == 8:
            self.wait(u, 7, n["c"])

    def wait(self, u, phase, size):
        for cp in self.pending.pop((u, phase), []):
            cp.wait_recv()

    pending = None


def make_exchange(*a):
    e = Exchange(*a)
    e.pending = {}
    orig = e.copy
    def copy(u, phase, step, src, dst, axis):
        cp = orig(u, phase, step, src, dst, axis)
        e.pending.setdefault((u, phase), []).append(cp)
        return cp
    e.copy = copy
    return e


def barrier(ring):
    sem = pltpu.get_barrier_semaphore()
    count = 0
    for axis, size in ring.sizes.items():
        for k in range(1, size):
            pl.semaphore_signal(sem, inc=1, device_id=ring.peer(axis, k), device_id_type=MESH)
            count += 1
    pl.semaphore_wait(sem, count)


def reduce_kernel(groups, replicas, units, lag, own_in, small_in, full, small_out, own, rc, r1, r2, r3, sm, send, recv, ssend, srecv):
    ring = Ring(groups, replicas)
    barrier(ring)
    ex = make_exchange(ring, own, full, rc, r1, r2, r3, send, recv, units)
    smalls = []
    axes = ["c", "x", "y", "z"]
    def small_send(p):
        ax = axes[p]
        n = ring.sizes[ax]
        src = sm.at[p, ring.at[ax]]
        cps = []
        for k in range(1, n):
            cp = pltpu.make_async_remote_copy(src_ref=src, dst_ref=src, send_sem=ssend.at[p, k - 1], recv_sem=srecv.at[p, k - 1],
                                              device_id=ring.peer(ax, k), device_id_type=MESH)
            cp.start(); cps.append(cp)
        smalls.append(cps)
    def small_add(p):
        ax = axes[p]
        for cp in smalls[p]:
            cp.wait_recv()
        total = sm[p, 0]
        for j in range(1, ring.sizes[ax]):
            total = total + sm[p, j]
        return total
    own[...] = own_in[...]
    sm[0, ring.at["c"]] = small_in[...]
    small_send(0)
    steps = 9
    for t in range(steps + lag * ((units - 1) // 2) ):
        for u in range(units):
            s = t - lag * (u // 2)
            if 0 <= s < steps:
                ex.start(u, s)
        if t < 3:
            v = small_add(t)
            sm[t + 1, ring.at[axes[t + 1]]] = v
            small_send(t + 1)
        elif t == 3:
            small_out[...] = small_add(3)
    for cps in smalls:
        for cp in cps:
            cp.wait_send()
    for cp in ex.tail:
        cp.wait_send()


def all_reduce(own, small, groups, replicas, lag=1):
    cores, nx, ny, nz = grid_of(groups, replicas)
    lead = cores * nx * ny
    units = own.shape[0] // lead
    nm = max(nx, ny)
    peers = max(cores, nx, ny, nz) - 1
    scratch = [
        pltpu.VMEM(own.shape, own.dtype),
        pltpu.VMEM((units, lead // cores, ROWS, LANES), own.dtype),
        pltpu.VMEM((units, nm - 1, nm, ROWS, LANES), own.dtype),
        pltpu.VMEM((units, nm - 1, ROWS, LANES), own.dtype),
        pltpu.VMEM((units, nz - 1, ROWS // nz, LANES), own.dtype),
        pltpu.VMEM((4, max(cores, nx, ny, nz)) + small.shape, jnp.float32),
        pltpu.SemaphoreType.DMA((units, 8, peers)),
        pltpu.SemaphoreType.DMA((units, 8, peers)),
        pltpu.SemaphoreType.DMA((4, peers)),
        pltpu.SemaphoreType.DMA((4, peers)),
    ]
    vm = pl.BlockSpec(memory_space=pltpu.VMEM)
    return pl.pallas_call(
        functools.partial(reduce_kernel, groups, replicas, units, lag),
        out_shape=(jax.ShapeDtypeStruct(own.shape, own.dtype), jax.ShapeDtypeStruct(small.shape, small.dtype)),
        in_specs=[vm, vm], out_specs=(vm, vm), scratch_shapes=scratch,
        compiler_params=pltpu.CompilerParams(collective_id=0, has_side_effects=True, vmem_limit_bytes=60 * 2**20),
        name="grad_sum",
    )(own, small)


def lanes_first(table):
    rows, columns = table.shape
    return table.reshape(rows, columns // LANES, LANES).transpose(1, 0, 2)


def lanes_last(blocks):
    count, rows, width = blocks.shape
    return blocks.transpose(1, 0, 2).reshape(rows, count * width)


def sum_gradients(grads, router_grad):
    gain_one, query, key, value, output, gain_two, gate, up, down = grads
    groups, replicas = lax.axis_size("grp"), lax.axis_size("rep")
    if groups * replicas == 1:
        return grads + (router_grad,)
    cores, nx, ny, nz = grid_of(groups, replicas)
    packed = jnp.concatenate(
        [
            lanes_first(part.astype(jnp.bfloat16))
            for part in (
                down.T,
                gate,
                up,
                jnp.concatenate([query, key], 1),
                jnp.concatenate([value, output], 1),
            )
        ],
        0,
    )
    count = packed.shape[0]
    pad = -count % (cores * nx * ny)
    packed = jnp.pad(packed, ((0, pad), (0, 0), (0, 0)))
    small = jnp.concatenate([gain_one[None], gain_two[None], router_grad], 0)
    small = jnp.pad(small, ((0, 3), (0, -small.shape[1] % LANES)))
    full, sums = all_reduce(packed, small, groups, replicas)
    full = full.astype(jnp.float32)
    wide = gate.shape[1] // LANES
    narrow = (query.shape[1] + key.shape[1]) // LANES
    at = [0, wide, 2 * wide, 3 * wide, 3 * wide + narrow, 3 * wide + 2 * narrow]
    parts = [lanes_last(full[a:b]) for a, b in zip(at[:-1], at[1:])]
    width = query.shape[0]
    sums = sums[:5, :width]
    return (
        sums[0],
        parts[3][:, : query.shape[1]],
        parts[3][:, query.shape[1] :],
        parts[4][:, : value.shape[1]],
        parts[4][:, value.shape[1] :],
        sums[1],
        parts[1],
        parts[2],
        parts[0].T,
        sums[2:5],
    )


def rms_scale(values):
    return lax.rsqrt(jnp.mean(values * values, axis=-1, keepdims=True) + EPSILON)


def exact_parts(values):
    upper = values.astype(jnp.bfloat16)
    rest = values - upper.astype(jnp.float32)
    middle_part = rest.astype(jnp.bfloat16)
    lowest = (rest - middle_part.astype(jnp.float32)).astype(jnp.bfloat16)
    return (upper, middle_part, lowest)


def pick_rows(whole, selector):
    parts = exact_parts(whole)
    taken = [
        jnp.einsum("sjp,spd->sjd", selector, piece, preferred_element_type=jnp.float32)
        for piece in parts
    ]
    return taken[0] + taken[1] + taken[2]


def place_rows(whole, selector, added):
    parts = exact_parts(added)
    spread = [
        jnp.einsum("sjp,sjd->spd", selector, piece, preferred_element_type=jnp.float32)
        for piece in parts
    ]
    return whole + (spread[0] + spread[1] + spread[2])


def rope_tables(positions):
    halfway = HEAD_DIM // 2
    inverse = ROPE_BASE ** (-(jnp.arange(halfway, dtype=jnp.float32) * (2.0 / HEAD_DIM)))
    angles = positions.astype(jnp.float32)[..., None] * inverse
    cosines = jnp.cos(angles)
    sine_values = jnp.sin(angles)
    return (
        jnp.concatenate([cosines, cosines], -1),
        jnp.concatenate([sine_values, sine_values], -1),
    )


def rotate(values, cosines, sine_values):
    halfway = values.shape[-1] // 2
    turned = jnp.concatenate([-values[..., halfway:], values[..., :halfway]], -1)
    return values * cosines + turned * sine_values


def unrotate(grads_in, cosines, sine_values):
    halfway = grads_in.shape[-1] // 2
    scaled = grads_in * sine_values
    return grads_in * cosines + jnp.concatenate([scaled[..., halfway:], -scaled[..., :halfway]], -1)


def attention_mask(labels, starts, positions, active):
    same_doc = (labels[:, :, None] == labels[:, None, :]) & (
        starts[:, :, None] == starts[:, None, :]
    )
    causal = positions[:, None, :] <= positions[:, :, None]
    length = labels.shape[1]
    return same_doc & causal & active[:, None, :] | jnp.eye(length, dtype=bool)[None]


def block_inner(rows_low, allowed, positions, weights, kept_lse):
    (
        attention_gain,
        query_weight,
        key_weight,
        value_weight,
        output_weight,
        feed_gain,
        gate_weight,
        up_weight,
        down_weight,
    ) = weights
    group_count, length, model_width = rows_low.shape
    kv_count = key_weight.shape[1] // HEAD_DIM
    per_group = query_weight.shape[1] // key_weight.shape[1]
    flat_rows = rows_low.reshape(group_count * length, model_width).astype(jnp.float32)
    inverse_one = rms_scale(flat_rows)
    normed_one = (flat_rows * inverse_one * attention_gain).astype(jnp.bfloat16)
    query_rows = jnp.dot(normed_one, query_weight, preferred_element_type=jnp.float32)
    key_pre = jnp.dot(normed_one, key_weight, preferred_element_type=jnp.float32)
    value_low = jnp.dot(normed_one, value_weight, preferred_element_type=jnp.float32).astype(
        jnp.bfloat16
    )
    cosines, sine_values = rope_tables(positions)
    query_low = rotate(
        query_rows.reshape(group_count, length, kv_count, per_group, HEAD_DIM),
        cosines[:, :, None, None],
        sine_values[:, :, None, None],
    ).astype(jnp.bfloat16)
    key_low = rotate(
        key_pre.reshape(group_count, length, kv_count, HEAD_DIM),
        cosines[:, :, None],
        sine_values[:, :, None],
    ).astype(jnp.bfloat16)
    value_low = value_low.reshape(group_count, length, kv_count, HEAD_DIM)
    scores = (
        jnp.einsum("gqkhd,gskd->gkhqs", query_low, key_low, preferred_element_type=jnp.float32)
        * SCORE_SCALE
    )
    scores = jnp.where(allowed[:, None, None], scores, MASKED)
    if kept_lse is None:
        highest = jnp.max(scores, axis=-1, keepdims=True)
        kept_lse = highest + jnp.log(jnp.sum(jnp.exp(scores - highest), axis=-1, keepdims=True))
    shares = jnp.exp(scores - kept_lse)
    shares_low = shares.astype(jnp.bfloat16)
    mixed_rows = jnp.einsum(
        "gkhqs,gskd->gqkhd", shares_low, value_low, preferred_element_type=jnp.float32
    )
    mixed_low = mixed_rows.reshape(group_count * length, model_width).astype(jnp.bfloat16)
    attended = jnp.dot(mixed_low, output_weight, preferred_element_type=jnp.float32)
    middle = flat_rows + attended
    inverse_two = rms_scale(middle)
    normed_two = (middle * inverse_two * feed_gain).astype(jnp.bfloat16)
    gate_pre = jnp.dot(normed_two, gate_weight, preferred_element_type=jnp.float32)
    up_pre = jnp.dot(normed_two, up_weight, preferred_element_type=jnp.float32)
    hidden = (jax.nn.silu(gate_pre) * up_pre).astype(jnp.bfloat16)
    return (
        flat_rows,
        inverse_one,
        normed_one,
        query_low,
        key_low,
        value_low,
        cosines,
        sine_values,
        shares,
        shares_low,
        mixed_low,
        attended,
        middle,
        inverse_two,
        normed_two,
        gate_pre,
        up_pre,
        hidden,
        kept_lse,
    )


def block_forward(rows_low, allowed, positions, weights):
    inner = block_inner(rows_low, allowed, positions, weights, None)
    attended = inner[11]
    hidden = inner[17]
    change = attended + jnp.dot(hidden, weights[8], preferred_element_type=jnp.float32)
    return (change, inner[18])


def block_backward(rows_low, allowed, positions, kept_lse, change_grad, weights):
    (
        attention_gain,
        query_weight,
        key_weight,
        value_weight,
        output_weight,
        feed_gain,
        gate_weight,
        up_weight,
        down_weight,
    ) = weights
    (
        flat_rows,
        inverse_one,
        normed_one,
        query_low,
        key_low,
        value_low,
        cosines,
        sine_values,
        shares,
        shares_low,
        mixed_low,
        attended,
        middle,
        inverse_two,
        normed_two,
        gate_pre,
        up_pre,
        hidden,
        kept_lse,
    ) = block_inner(rows_low, allowed, positions, weights, kept_lse)
    group_count, length, model_width = rows_low.shape
    kv_count = key_weight.shape[1] // HEAD_DIM
    per_group = query_weight.shape[1] // key_weight.shape[1]
    change_flat = change_grad.reshape(group_count * length, model_width)
    grad_down = jnp.einsum("rf,rd->fd", hidden, change_flat, preferred_element_type=jnp.float32)
    hidden_grad = jnp.einsum(
        "rd,fd->rf", change_flat, down_weight, preferred_element_type=jnp.float32
    )
    gate_sigmoid = jax.nn.sigmoid(gate_pre)
    gate_grad = (
        hidden_grad * up_pre * (gate_sigmoid + gate_pre * gate_sigmoid * (1.0 - gate_sigmoid))
    ).astype(jnp.bfloat16)
    up_grad = (hidden_grad * gate_pre * gate_sigmoid).astype(jnp.bfloat16)
    grad_gate = jnp.einsum("rd,rf->df", normed_two, gate_grad, preferred_element_type=jnp.float32)
    grad_up = jnp.einsum("rd,rf->df", normed_two, up_grad, preferred_element_type=jnp.float32)
    normed_two_grad = jnp.einsum(
        "rf,df->rd", gate_grad, gate_weight, preferred_element_type=jnp.float32
    ) + jnp.einsum("rf,df->rd", up_grad, up_weight, preferred_element_type=jnp.float32)
    scaled_two = middle * inverse_two
    grad_feed_gain = jnp.sum(normed_two_grad * scaled_two, axis=0)
    upstream_two = normed_two_grad * feed_gain
    middle_grad = inverse_two * (
        upstream_two - scaled_two * jnp.mean(upstream_two * scaled_two, axis=-1, keepdims=True)
    )
    attended_grad = (change_flat.astype(jnp.float32) + middle_grad).astype(jnp.bfloat16)
    grad_output = jnp.einsum(
        "rc,rd->cd", mixed_low, attended_grad, preferred_element_type=jnp.float32
    )
    mixed_grad = jnp.einsum(
        "rd,cd->rc", attended_grad, output_weight, preferred_element_type=jnp.float32
    ).astype(jnp.bfloat16)
    mixed_grad = mixed_grad.reshape(group_count, length, kv_count, per_group, HEAD_DIM)
    prob_grad = jnp.einsum(
        "gqkhd,gskd->gkhqs", mixed_grad, value_low, preferred_element_type=jnp.float32
    )
    value_sum = jnp.einsum(
        "gkhqs,gqkhd->gskd", shares_low, mixed_grad, preferred_element_type=jnp.float32
    )
    score_grad = (
        shares * (prob_grad - jnp.sum(shares * prob_grad, axis=-1, keepdims=True))
    ).astype(jnp.bfloat16)
    query_back = (
        jnp.einsum("gkhqs,gskd->gqkhd", score_grad, key_low, preferred_element_type=jnp.float32)
        * SCORE_SCALE
    )
    key_back = (
        jnp.einsum("gkhqs,gqkhd->gskd", score_grad, query_low, preferred_element_type=jnp.float32)
        * SCORE_SCALE
    )
    query_grad = (
        unrotate(query_back, cosines[:, :, None, None], sine_values[:, :, None, None])
        .astype(jnp.bfloat16)
        .reshape(group_count * length, model_width)
    )
    key_grad = (
        unrotate(key_back, cosines[:, :, None], sine_values[:, :, None])
        .astype(jnp.bfloat16)
        .reshape(group_count * length, kv_count * HEAD_DIM)
    )
    value_grad = value_sum.astype(jnp.bfloat16).reshape(group_count * length, kv_count * HEAD_DIM)
    grad_query = jnp.einsum("rd,rc->dc", normed_one, query_grad, preferred_element_type=jnp.float32)
    grad_key = jnp.einsum("rd,rc->dc", normed_one, key_grad, preferred_element_type=jnp.float32)
    grad_value = jnp.einsum("rd,rc->dc", normed_one, value_grad, preferred_element_type=jnp.float32)
    normed_one_grad = (
        jnp.einsum("rc,dc->rd", query_grad, query_weight, preferred_element_type=jnp.float32)
        + jnp.einsum("rc,dc->rd", key_grad, key_weight, preferred_element_type=jnp.float32)
        + jnp.einsum("rc,dc->rd", value_grad, value_weight, preferred_element_type=jnp.float32)
    )
    scaled_one = flat_rows * inverse_one
    grad_attention_gain = jnp.sum(normed_one_grad * scaled_one, axis=0)
    upstream_one = normed_one_grad * attention_gain
    rows_grad = middle_grad + inverse_one * (
        upstream_one - scaled_one * jnp.mean(upstream_one * scaled_one, axis=-1, keepdims=True)
    )
    return (
        rows_grad,
        (
            grad_attention_gain,
            grad_query,
            grad_key,
            grad_value,
            grad_output,
            grad_feed_gain,
            grad_gate,
            grad_up,
            grad_down,
        ),
    )


TILE = 192
FLOAT = jnp.float32
LOW = jnp.bfloat16
VMEM_MOST = 63 * 2**20
FAR = 1.0e6


def dot_nn(a, b):
    return lax.dot_general(a, b, (((1,), (0,)), ((), ())), preferred_element_type=FLOAT)


def dot_nt(a, b):
    return lax.dot_general(a, b, (((1,), (1,)), ((), ())), preferred_element_type=FLOAT)


def dot_tn(a, b):
    return lax.dot_general(a, b, (((0,), (0,)), ((), ())), preferred_element_type=FLOAT)


def spans(width, step=256):
    return [(a, min(a + step, width)) for a in range(0, width, step)]


def turn_constants():
    exact = (10000.0 ** (-np.arange(HEAD_DIM // 2) * (2.0 / HEAD_DIM))) / (2.0 * np.pi)
    scale = 2.0 ** (11 - np.floor(np.log2(exact)))
    upper = np.round(exact * scale) / scale
    rows = np.zeros((8, LANES), np.float32)
    rows[0] = np.tile(upper, LANES // upper.size)
    rows[1] = np.tile(exact - upper, LANES // upper.size)
    return rows


def series(t, terms):
    square = t * t
    total = jnp.full_like(t, terms[-1])
    for term in terms[-2::-1]:
        total = total * square + term
    return total


TWO_PI = 2.0 * np.pi
COS_TERMS = [float((-1) ** i * TWO_PI ** (2 * i) / math.factorial(2 * i)) for i in range(11)]
SIN_TERMS = [float((-1) ** i * TWO_PI ** (2 * i + 1) / math.factorial(2 * i + 1)) for i in range(11)]


def lane_of(shape):
    return lax.broadcasted_iota(jnp.int32, shape, len(shape) - 1)


def row_of(shape):
    return lax.broadcasted_iota(jnp.int32, shape, len(shape) - 2)


def rotary(position, turns):
    coarse = position * turns[0:1, :]
    coarse = coarse - jnp.floor(coarse + 0.5)
    whole = coarse + position * turns[1:2, :]
    t = whole - jnp.floor(whole + 0.5)
    sine = series(t, SIN_TERMS) * t
    lower = lane_of(t.shape) % HEAD_DIM < HEAD_DIM // 2
    return series(t, COS_TERMS), jnp.where(lower, -sine, sine)


def turned(v):
    lower = lane_of(v.shape) % HEAD_DIM < HEAD_DIM // 2
    return jnp.where(lower, pltpu.roll(v, LANES - HEAD_DIM // 2, 1), pltpu.roll(v, HEAD_DIM // 2, 1))


def logistic(v):
    return 1.0 / (1.0 + jnp.exp(-v))


def halves(v):
    lower = lane_of(v.shape) < HEAD_DIM
    first, second = jnp.where(lower, v, 0.0), jnp.where(lower, 0.0, v)
    return [
        [first.astype(LOW), pltpu.roll(first, HEAD_DIM, 1).astype(LOW)],
        [pltpu.roll(second, HEAD_DIM, 1).astype(LOW), second.astype(LOW)],
    ]


class Names:
    pass


def load_rope_keys(n, rows):
    four = halves(n.qk[rows, 512:640].astype(FLOAT))
    five = halves(n.qk[rows, 640:768].astype(FLOAT))
    keys = [four[1], five[0], five[1]]
    zero = halves(n.vv[rows, 0:128].astype(FLOAT))
    one = halves(n.vv[rows, 128:256].astype(FLOAT))
    return keys, [zero[0], zero[1], one[1]]


def forward_tile(n, t, level):
    rows = pl.ds(pl.multiple_of(t * TILE, TILE), TILE)
    x = n.st[rows, :]
    gate = logistic(jnp.sum(x * n.router[pl.ds(level, 1), :], axis=1, keepdims=True))
    sent = x.astype(LOW).astype(FLOAT)
    width = sent.shape[1]
    inv1 = lax.rsqrt(jnp.sum(sent * sent, axis=1, keepdims=True) * (1.0 / width) + EPSILON)
    n.z1[rows, :] = (sent * inv1 * n.gains[0:1, :]).astype(LOW)
    cosine, sine = n.ctab[rows, :], n.stab[rows, :]
    for a, b in spans(768):
        part = dot_nn(n.z1[rows, :], n.wqk[:, a:b])
        for c in range(0, b - a, LANES):
            v = part[:, c : c + LANES]
            n.qk[rows, a + c : a + c + LANES] = (v * cosine + turned(v) * sine).astype(LOW)
    n.vv[rows, :] = dot_nn(n.z1[rows, :], n.wvv[...]).astype(LOW)
    keys, values = load_rope_keys(n, rows)
    own = n.aux[rows, 0:1]
    low_end = n.aux[rows, 1:2]
    eye = row_of((TILE, TILE)) == lane_of((TILE, TILE))
    other = jnp.sum(jnp.where(eye, own, 0.0), axis=0, keepdims=True)
    bias = jnp.where((other <= own) & (other >= low_end), 0.0, MASKED)
    heads = width // HEAD_DIM
    for pair in range((heads + 1) // 2):
        query = n.qk[rows, pair * LANES : (pair + 1) * LANES]
        total = None
        for half in range(2):
            head = 2 * pair + half
            if head >= heads:
                continue
            scores = dot_nt(query, keys[head // 3][half]) * SCORE_SCALE + bias
            top = jnp.max(scores, axis=1, keepdims=True)
            weight = jnp.exp(scores - top)
            share = (weight * (1.0 / jnp.sum(weight, axis=1, keepdims=True))).astype(LOW)
            n.share[t, head] = share
            mix = dot_nn(share, values[head // 3][half])
            total = mix if total is None else total + mix
        if 2 * pair + 1 < heads:
            n.mixed[rows, pair * LANES : (pair + 1) * LANES] = total.astype(LOW)
        else:
            n.mixed[rows, pair * LANES : width] = total[:, :HEAD_DIM].astype(LOW)
    for a, b in spans(width):
        n.attended[:, a:b] = dot_nn(n.mixed[rows, :], n.wo[:, a:b])
    middle = sent + n.attended[...]
    inv2 = lax.rsqrt(jnp.sum(middle * middle, axis=1, keepdims=True) * (1.0 / width) + EPSILON)
    t2 = middle * inv2
    n.t2[rows, :] = t2.astype(LOW)
    n.z2[rows, :] = (t2 * n.gains[1:2, :]).astype(LOW)
    lane = lane_of((TILE, LANES))
    aux = n.aux[rows, :]
    aux = jnp.where(lane == 3, gate, jnp.where(lane == 4, inv2, jnp.where(lane == 5, inv1, aux)))
    n.aux[rows, :] = aux
    for a, b in spans(n.wg.shape[1]):
        pre = dot_nn(n.z2[rows, :], n.wg[:, a:b])
        up = dot_nn(n.z2[rows, :], n.wu[:, a:b])
        n.gg[rows, a:b] = pre.astype(LOW)
        n.ug[rows, a:b] = up.astype(LOW)
        n.hidden[rows, a:b] = (pre * logistic(pre) * up).astype(LOW)
    active = aux[:, 2:3]
    for a, b in spans(width):
        change = (n.attended[:, a:b] + dot_nt(n.hidden[rows, :], n.wd[a:b, :])).astype(LOW)
        n.change[rows, a:b] = change
        n.tile[:, a:b] = n.st[rows, a:b] + (gate * active) * change.astype(FLOAT)


def backward_tile(n, t, level):
    rows = pl.ds(pl.multiple_of(t * TILE, TILE), TILE)
    width = n.tile.shape[1]
    aux = n.aux[rows, :]
    active, gate, inv2, inv1 = aux[:, 2:3], aux[:, 3:4], aux[:, 4:5], aux[:, 5:6]
    grad = n.tile[...]
    n.cg[rows, :] = (gate * active * grad).astype(LOW)
    logit = (
        jnp.sum(grad * n.change[rows, :].astype(FLOAT), axis=1, keepdims=True)
        * active * gate * (1.0 - gate)
    )
    x = n.st[rows, :].astype(FLOAT)
    at = pl.ds(level, 1)
    n.small[pl.ds(2 + level, 1), 0:width] += jnp.sum(logit * x, axis=0, keepdims=True)
    n.tile[...] = grad + (active * logit) * n.router[at, :]
    for a, b in spans(n.wg.shape[1]):
        back = dot_nn(n.cg[rows, :], n.wd[:, a:b])
        pre = n.gg[rows, a:b].astype(FLOAT)
        up = n.ug[rows, a:b].astype(FLOAT)
        share = logistic(pre)
        n.gg[rows, a:b] = (back * up * (share + pre * share * (1.0 - share))).astype(LOW)
        n.ug[rows, a:b] = (back * pre * share).astype(LOW)
    for a, b in spans(width):
        n.attended[:, a:b] = dot_nt(n.gg[rows, :], n.wg[a:b, :]) + dot_nt(n.ug[rows, :], n.wu[a:b, :])
    z2_grad = n.attended[...]
    t2 = n.t2[rows, :].astype(FLOAT)
    n.small[1:2, 0:width] += jnp.sum(z2_grad * t2, axis=0, keepdims=True)
    lifted = z2_grad * n.gains[1:2, :]
    mean = jnp.sum(lifted * t2, axis=1, keepdims=True) * (1.0 / width)
    middle_grad = inv2 * (lifted - t2 * mean)
    n.attended[...] = middle_grad
    n.ag[rows, 0:width] = (n.cg[rows, :].astype(FLOAT) + middle_grad).astype(LOW)
    n.ag[rows, width:] = jnp.zeros((TILE, n.ag.shape[1] - width), LOW)
    for a, b in spans(width):
        n.dm[:, a:b] = dot_nt(n.ag[rows, 0:width], n.wo[a:b, :]).astype(LOW)
    n.dm[:, width:] = jnp.zeros((TILE, n.dm.shape[1] - width), LOW)
    keys, values = load_rope_keys(n, rows)
    heads = width // HEAD_DIM
    key_part = [[None, None] for _ in range(3)]
    value_part = [[None, None] for _ in range(3)]
    cosine, sine = n.ctab[rows, :], n.stab[rows, :]

    def plus(a, b):
        return b if a is None else a + b

    def unturned(v):
        v = v * SCORE_SCALE
        return (v * cosine - turned(v) * sine).astype(LOW)

    last = None
    for pair in range((heads + 1) // 2):
        columns = slice(pair * LANES, (pair + 1) * LANES)
        query = n.qk[rows, columns]
        mixed_grad = n.dm[:, columns]
        total = None
        for half in range(2):
            head = 2 * pair + half
            if head >= heads:
                continue
            g = head // 3
            share_low = n.share[t, head]
            share = share_low.astype(FLOAT)
            back = dot_nt(mixed_grad, values[g][half])
            inner = jnp.sum(share * back, axis=1, keepdims=True)
            score = (share * (back - inner)).astype(LOW)
            total = plus(total, dot_nn(score, keys[g][half]))
            key_part[g][half] = plus(key_part[g][half], dot_tn(score, query))
            value_part[g][half] = plus(value_part[g][half], dot_tn(share_low, mixed_grad))
        if 2 * pair + 1 < heads:
            n.dqk[rows, columns] = unturned(total)
        else:
            last = total
    lower = lane_of((TILE, LANES)) < HEAD_DIM

    def joined(part, where):
        first, second = part
        if where == 0:
            return jnp.where(lower, first + pltpu.roll(second, HEAD_DIM, 1), 0.0)
        return jnp.where(lower, 0.0, pltpu.roll(first, HEAD_DIM, 1) + second)

    n.dqk[rows, 512:640] = unturned(jnp.where(lower, last, 0.0) + joined(key_part[0], 1))
    n.dqk[rows, 640:768] = unturned(joined(key_part[1], 0) + joined(key_part[2], 1))
    n.dvv[rows, 0:128] = (joined(value_part[0], 0) + joined(value_part[1], 1)).astype(LOW)
    n.dvv[rows, 128:256] = joined(value_part[2], 1).astype(LOW)
    sent = n.st[rows, :].astype(LOW).astype(FLOAT)
    t1 = sent * inv1
    mean = jnp.zeros((TILE, 1), FLOAT)
    for a, b in spans(width):
        z1_grad = dot_nt(n.dqk[rows, :], n.wqk[a:b, :]) + dot_nt(n.dvv[rows, :], n.wvv[a:b, :])
        n.small[0:1, a:b] += jnp.sum(z1_grad * t1[:, a:b], axis=0, keepdims=True)
        lifted = z1_grad * n.gains[0:1, a:b]
        mean = mean + jnp.sum(lifted * t1[:, a:b], axis=1, keepdims=True)
        n.lift[:, a:b] = lifted
    mean = mean * (1.0 / width)
    sent_grad = (n.attended[...] + inv1 * (n.lift[...] - t1 * mean)).astype(LOW).astype(FLOAT)
    n.tile[...] += active * sent_grad


def level_of(t, seqs):
    return jnp.where(t < seqs, 0, jnp.where(t < seqs + seqs // 2, 1, 2))


def each_level(t, seqs, body):
    first = 0
    for level in range(NREC):
        count = seqs >> level

        @pl.when((t >= first) & (t < first + count))
        def _(level=level, first=first):
            body(level, t - first, 1 << level, TILE >> level)

        first += count


def rows_at(start, size, align=16):
    return pl.ds(pl.multiple_of(start, align), size)


def index_rows(n, g, s, counts, ends):
    eye = row_of((TILE, TILE)) == lane_of((TILE, TILE))
    before = lane_of((TILE, TILE)) < row_of((TILE, TILE))
    first = n.picks[0][g, s : s + 1, :].astype(FLOAT)

    def column(row):
        return jnp.sum(jnp.where(eye, row, 0.0), axis=1, keepdims=True)

    def as_row(col):
        return jnp.sum(jnp.where(eye, col, 0.0), axis=0, keepdims=True)

    first_col = column(first)
    index = row_of((TILE, 1))
    live = index < counts[0]
    depth = jnp.where(live, 2.0, 3.0)
    for level in (1, 2):
        picked = n.picks[level][g, s : s + 1, :].astype(FLOAT)
        match = (first_col == picked) & (lane_of(picked.shape) < counts[level])
        inside = jnp.max(jnp.where(match, 1.0, 0.0), axis=1, keepdims=True)
        depth = jnp.where(live & (inside > 0.5), 2.0 - level, depth)
    depth_row = as_row(depth)
    ahead = (depth_row < depth) | ((depth_row == depth) & before)
    new = jnp.sum(jnp.where(ahead, 1.0, 0.0), axis=1, keepdims=True)
    new_row = as_row(new)
    line, lane = row_of((TILE, TILE)).astype(FLOAT), lane_of((TILE, TILE)).astype(FLOAT)
    spot = jnp.sum(jnp.where(new_row == line, first, 0.0), axis=1, keepdims=True)
    spot_row = jnp.sum(jnp.where(new == lane, first_col, 0.0), axis=0, keepdims=True)
    spot_row = jnp.where(lane_of(spot_row.shape) < counts[0], spot_row, -1.0)
    start = jnp.zeros_like(spot)
    for document in range(len(ends)):
        start = jnp.where(spot >= ends[document], ends[document], start)
    ctab, stab = rotary(spot, n.turns[...])
    lane_aux = lane_of((TILE, LANES))
    shift = s * 4096.0
    for level in range(NREC):
        size = TILE >> level
        at = rows_at(sum(n.seqs >> k for k in range(level)) * TILE + s * size, size)
        active = index[:size] < counts[level]
        key = jnp.where(active, spot[:size] + shift, FAR + s * 4096.0 + index[:size].astype(FLOAT))
        low = jnp.where(active, start[:size] + shift, key)
        aux = jnp.where(lane_aux[:size] == 0, key, jnp.where(lane_aux[:size] == 1, low, jnp.where(active, 1.0, 0.0)))
        n.aux[at, :] = aux
        n.ctab[at, :] = ctab[:size]
        n.stab[at, :] = stab[:size]
    n.places[s : s + 1, :] = spot_row
    return spot, live


def start_copies(copies):
    for copy in copies:
        copy.start()


def transpose_into(dst, src):
    rows, width = src.shape
    for a, b in spans(rows, LANES):
        dst[0:width, a:b] = src[a:b, :].T


def block_kernel(
    names, seqs, *refs
):
    n = Names()
    for name, ref in zip(names, refs):
        setattr(n, name, ref)
    n.seqs = seqs
    n.picks = (n.picks_first, n.picks_second, n.picks_third)
    g = lax.axis_index("grp")
    tiles = seqs + seqs // 2 + seqs // 4
    width, length = n.tokens.shape[1:]
    weight_copies = {}
    for i, (src, dst) in enumerate(
        [("query", "wq_in"), ("key", "wk_in"), ("value", "wv_in"), ("output", "wo"), ("gate", "wg"), ("up", "wu"), ("down", "wd")]
    ):
        weight_copies[dst] = pltpu.make_async_copy(getattr(n, src), getattr(n, dst), n.wsem.at[i])

    def fetch(src, s, slot):
        return pltpu.make_async_copy(src.at[s], n.inbox.at[slot], n.insem.at[slot])

    fetch(n.tokens, 0, 0).start()
    fetch(n.out_grad, 0, 1).start()
    start_copies(weight_copies.values())
    n.small[...] = jnp.zeros_like(n.small)
    n.gains[0:1, :] = n.gain_one[...].astype(FLOAT)
    n.gains[1:2, :] = n.gain_two[...].astype(FLOAT)
    n.router[0:NREC, :] = n.router_in[...].astype(FLOAT)
    for s in range(seqs):
        counts = [n.routes[g, s, level, 0] for level in range(NREC)]
        ends, total = [], 0
        for document in range(n.doc_lengths.shape[2]):
            total = total + n.doc_lengths[g, s, document]
            ends.append(total.astype(FLOAT))
        spot, live = index_rows(n, g, s, counts, ends)
        hit = (spot.astype(jnp.int32) == lane_of((TILE, length))) & live
        n.pick[...] = jnp.where(hit, 1.0, 0.0).astype(LOW)
        for slot, (src, dst) in enumerate(((n.tokens, n.st), (n.out_grad, n.gr))):
            fetch(src, s, slot).wait()
            for a, b in spans(width):
                dst[s * TILE : (s + 1) * TILE, a:b] = dot_nt(n.pick[...], n.inbox[slot, a:b, :]).astype(dst.dtype)
            if s + 1 < seqs:
                fetch(src, s + 1, slot).start()
    fetch(n.tokens, 0, 0).start()
    for copy in weight_copies.values():
        copy.wait()
    n.wqk[:, 0:512] = n.wq_in[:, 0:512]
    key32 = n.wk_in[...].astype(FLOAT).T
    n.wqk[:, 512:640] = jnp.concatenate([n.wq_in[:, 512:576].astype(FLOAT), key32[:, 0:64]], 1).astype(LOW)
    n.wqk[:, 640:768] = key32[:, 64:192].astype(LOW)
    value32 = n.wv_in[...].astype(FLOAT).T
    n.wvv[:, 0:128] = value32[:, 0:128].astype(LOW)
    n.wvv[:, 128:256] = jnp.concatenate([jnp.zeros((width, 64), FLOAT), value32[:, 128:192]], 1).astype(LOW)

    def forward_step(t, carry):
        level = level_of(t, seqs)
        forward_tile(n, t, level)

        def hand_on(level, tile, count, size):
            base = sum(seqs >> k for k in range(level + 1)) * TILE
            for k in range(count):
                s = tile * count + k
                n.fin[rows_at(s * TILE, size), :] = n.tile[k * size : (k + 1) * size, :].astype(LOW)
                if level + 1 < NREC:
                    n.st[rows_at(base + s * (size // 2), size // 2), :] = n.tile[k * size : k * size + size // 2, :]

        each_level(t, seqs, hand_on)
        return carry

    lax.fori_loop(0, tiles, forward_step, 0)
    sends = []
    for s in range(seqs):
        slot = s % 2
        fetch(n.tokens, s, slot).wait()
        if s + 1 < seqs:
            if s >= 1:
                sends[s - 1].wait()
            fetch(n.tokens, s + 1, 1 - slot).start()
        place_rows_into(n.inbox.at[slot], n.fin, s, n.places)
        copy = pltpu.make_async_copy(n.inbox.at[slot], n.out_state.at[s], n.outsem.at[slot])
        copy.start()
        sends.append(copy)
    def backward_step(i, carry):
        t = tiles - 1 - i
        level = level_of(t, seqs)

        def take(level, tile, count, size):
            for k in range(count):
                s = tile * count + k
                n.tile[k * size : (k + 1) * size, :] = n.gr[rows_at(s * TILE, size), :]

        def give(level, tile, count, size):
            for k in range(count):
                s = tile * count + k
                n.gr[rows_at(s * TILE, size), :] = n.tile[k * size : (k + 1) * size, :]

        each_level(t, seqs, take)
        backward_tile(n, t, level)
        each_level(t, seqs, give)
        return carry

    lax.fori_loop(0, tiles, backward_step, 0)
    n.grad_rows[...] = n.gr[...].astype(LOW)
    n.places_out[...] = n.places[...]
    n.small_out[...] = n.small[...]
    def emit(left, right, first, blocks):
        def body(i, carry):
            part = dot_nn(left[0:width, :], right[:, pl.ds(pl.multiple_of(i * 256, 256), 256)])
            slot = i % 2
            at = first + 2 * i

            @pl.when(i >= 2)
            def _():
                pltpu.make_async_copy(n.stage.at[slot], n.packed.at[pl.ds(at - 4, 2)], n.gsem.at[slot]).wait()

            n.stage[slot, 0] = part[:, 0:128].astype(LOW)
            n.stage[slot, 1] = part[:, 128:256].astype(LOW)
            pltpu.make_async_copy(n.stage.at[slot], n.packed.at[pl.ds(at, 2)], n.gsem.at[slot]).start()
            return carry

        lax.fori_loop(0, blocks // 2, body, 0)
        for i in range(max(0, blocks // 2 - 2), blocks // 2):
            pltpu.make_async_copy(n.stage.at[i % 2], n.packed.at[pl.ds(first + 2 * i, 2)], n.gsem.at[i % 2]).wait()

    wide = n.wg.shape[1] // LANES
    transpose_into(n.left, n.cg)
    emit(n.left, n.hidden, 0, wide)
    transpose_into(n.left, n.z2)
    emit(n.left, n.gg, wide, wide)
    emit(n.left, n.ug, 2 * wide, wide)
    transpose_into(n.left, n.z1)
    emit(n.left, n.dqk, 3 * wide, 6)
    tail = dot_nn(n.left[0:width, :], n.dvv[:, 128:256])
    n.stage[0, 1] = dot_nn(n.left[0:width, :], n.dvv[:, 0:128]).astype(LOW)
    transpose_into(n.left, n.mixed)
    n.stage[0, 0] = (tail + dot_nn(n.left[0:width, :], n.ag[:, 512:640])).astype(LOW)
    copy = pltpu.make_async_copy(n.stage.at[0], n.packed.at[pl.ds(3 * wide + 10, 2)], n.gsem.at[0])
    copy.start()
    copy.wait()
    emit(n.left, n.ag, 3 * wide + 6, 4)
    for s in range(max(0, seqs - 2), seqs):
        sends[s].wait()


def place_rows_into(box, fin, s, places):
    width, length = box.shape
    eye = row_of((TILE, TILE)) == lane_of((TILE, TILE))
    where = jnp.sum(jnp.where(eye, places[s : s + 1, :], 0.0), axis=1, keepdims=True).astype(jnp.int32)
    for a, b in spans(length):
        hit = lane_of((TILE, b - a)) + a == where
        mark = jnp.where(hit, 1.0, 0.0)
        any_hit = jnp.max(mark, axis=0, keepdims=True) > 0.5
        low = mark.astype(LOW)
        placed = dot_tn(fin[s * TILE : (s + 1) * TILE, :], low)
        box[:, a:b] = jnp.where(any_hit, placed, box[:, a:b].astype(FLOAT)).astype(LOW)


def block_call(tokens, weights, out_grad, doc_lengths, picks, routes):
    seqs, width, length = tokens.shape
    (gain_one, query, key, value, output, gain_two, gate, up, down, router) = weights
    rows = seqs * TILE * 7 // 4
    front = seqs * TILE
    inner = gate.shape[1]
    hbm, vm, sm = (pl.BlockSpec(memory_space=m) for m in (pl.ANY, pltpu.VMEM, pltpu.SMEM))
    ins = [
        ("tokens", tokens, hbm), ("out_grad", out_grad, hbm), ("query", query, hbm), ("key", key, hbm),
        ("value", value, hbm), ("output", output, hbm), ("gate", gate, hbm), ("up", up, hbm), ("down", down, hbm),
        ("gain_one", gain_one, vm), ("gain_two", gain_two, vm), ("router_in", router, vm), ("turns", jnp.asarray(turn_constants()), vm),
        ("doc_lengths", doc_lengths, sm), ("picks_first", picks[0], vm), ("picks_second", picks[1], vm),
        ("picks_third", picks[2], vm), ("routes", routes, sm),
    ]
    blocks = 3 * inner // LANES + 12
    outs = [
        ("out_state", tokens.shape, LOW, hbm), ("grad_rows", (front, width), LOW, vm),
        ("places_out", (8, TILE), FLOAT, vm), ("small_out", (8, 640), FLOAT, vm),
        ("packed", (blocks, width, LANES), LOW, hbm),
    ]
    scratch = [
        ("wq_in", (width, width), LOW), ("wk_in", key.shape, LOW), ("wv_in", value.shape, LOW),
        ("wqk", (width, 768), LOW), ("wvv", (width, 256), LOW), ("wo", output.shape, LOW),
        ("wg", gate.shape, LOW), ("wu", up.shape, LOW), ("wd", down.shape, LOW),
        ("inbox", (2, width, length), LOW), ("pick", (TILE, length), LOW),
        ("st", (rows, width), FLOAT), ("gr", (front, width), FLOAT), ("fin", (front, width), LOW),
        ("aux", (rows, LANES), FLOAT), ("ctab", (rows, LANES), FLOAT), ("stab", (rows, LANES), FLOAT),
        ("places", (8, TILE), FLOAT), ("small", (8, 640), FLOAT),
        ("gains", (8, width), FLOAT), ("router", (8, width), FLOAT),
        ("tile", (TILE, width), FLOAT), ("attended", (TILE, width), FLOAT), ("lift", (TILE, width), FLOAT),
        ("dm", (TILE, 640), LOW), ("z1", (rows, width), LOW), ("z2", (rows, width), LOW), ("t2", (rows, width), LOW),
        ("mixed", (rows, width), LOW), ("cg", (rows, width), LOW), ("ag", (rows, 640), LOW),
        ("change", (rows, width), LOW), ("qk", (rows, 768), LOW), ("vv", (rows, 256), LOW),
        ("dqk", (rows, 768), LOW), ("dvv", (rows, 256), LOW), ("hidden", (rows, inner), LOW),
        ("gg", (rows, inner), LOW), ("ug", (rows, inner), LOW), ("share", (rows // TILE, width // HEAD_DIM, TILE, TILE), LOW),
        ("left", (width, rows), LOW), ("stage", (2, 2, width, LANES), LOW),
    ]
    sems = [("wsem", 7), ("insem", 2), ("outsem", 2), ("gsem", 2)]
    names = [i[0] for i in ins] + [o[0] for o in outs] + [s[0] for s in scratch] + [s[0] for s in sems]
    return pl.pallas_call(
        functools.partial(block_kernel, names, seqs),
        out_shape=tuple(jax.ShapeDtypeStruct(o[1], o[2]) for o in outs),
        in_specs=[i[2] for i in ins],
        out_specs=tuple(o[3] for o in outs),
        scratch_shapes=[pltpu.VMEM(s[1], s[2]) for s in scratch] + [pltpu.SemaphoreType.DMA((s[1],)) for s in sems],
        compiler_params=pltpu.CompilerParams(vmem_limit_bytes=VMEM_MOST),
        name="recursions",
    )(*[i[1] for i in ins])


def finish_kernel(names, seqs, *refs):
    n = Names()
    for name, ref in zip(names, refs):
        setattr(n, name, ref)
    width = n.out_grad.shape[1]
    blocks = n.packed.shape[0]
    group = 4
    loads = [
        pltpu.make_async_copy(n.packed.at[pl.ds(i, group)], n.blocks.at[pl.ds(i, group)], n.bsem.at[i // group])
        for i in range(0, blocks, group)
    ]
    boxes = [pltpu.make_async_copy(n.out_grad.at[s], n.inbox.at[s], n.insem.at[s]) for s in range(seqs)]
    loads[0].start()
    for copy in boxes:
        copy.start()
    for copy in loads[1:]:
        copy.start()
    sends = []

    def send(src, dst):
        copy = pltpu.make_async_copy(src, dst, n.outsem.at[len(sends)])
        copy.start()
        sends.append(copy)

    ready = [0]

    def need(last):
        while ready[0] < -(-last // group):
            loads[ready[0]].wait()
            ready[0] += 1

    def place(s):
        boxes[s].wait()
        place_rows_into(n.inbox.at[s], n.grad_rows, s, n.places)
        send(n.inbox.at[s], n.grad_tokens.at[s])

    wide = n.gate.shape[1] // LANES
    for i in range(wide):
        need(i + 1)
        n.down_box[:, i * LANES : (i + 1) * LANES] = n.blocks[i].astype(FLOAT)
    send(n.down_box, n.down)
    place(0)
    for k, (box, out) in enumerate(((n.gate_box, n.gate), (n.up_box, n.up))):
        first = (k + 1) * wide
        for i in range(wide):
            need(first + i + 1)
            box[:, i * LANES : (i + 1) * LANES] = n.blocks[first + i].astype(FLOAT)
        send(box, out)
        place(k + 1)
    first = 3 * wide
    need(blocks)
    for base, box in ((first, n.query_box), (first + 6, n.output_box)):
        for i in range(4):
            box[:, i * LANES : (i + 1) * LANES] = n.blocks[base + i].astype(FLOAT)
        box[:, 512:576] = n.blocks[base + 4, :, 0:64].astype(FLOAT)
    send(n.query_box, n.query)
    send(n.output_box, n.output)
    n.key_box[0:64, :] = n.blocks[first + 4].astype(FLOAT).T[64:128, :]
    n.key_box[64:192, :] = n.blocks[first + 5].astype(FLOAT).T
    send(n.key_box, n.key)
    n.value_box[0:128, :] = n.blocks[first + 11].astype(FLOAT).T
    n.value_box[128:192, :] = n.blocks[first + 10].astype(FLOAT).T[64:128, :]
    send(n.value_box, n.value)
    for s in range(3, seqs):
        place(s)
    n.gain_one[...] = n.small[0:1, 0:width]
    n.gain_two[...] = n.small[1:2, 0:width]
    n.router[...] = n.small[2 : 2 + NREC, 0:width]
    for copy in sends:
        copy.wait()


def finish_call(out_grad, grad_rows, places, packed, small, shapes):
    seqs, width, length = out_grad.shape
    hbm, vm = (pl.BlockSpec(memory_space=m) for m in (pl.ANY, pltpu.VMEM))
    ins = [("out_grad", out_grad, hbm), ("grad_rows", grad_rows, vm), ("places", places, vm), ("packed", packed, hbm), ("small", small, vm)]
    outs = [("grad_tokens", out_grad.shape, LOW, hbm)]
    big = ("query", "key", "value", "output", "gate", "up", "down")
    outs += [(name, shapes[name], FLOAT, hbm) for name in big]
    outs += [("gain_one", (1, width), FLOAT, vm), ("gain_two", (1, width), FLOAT, vm), ("router", (NREC, width), FLOAT, vm)]
    blocks = 3 * shapes["gate"][1] // LANES + 12
    scratch = [("inbox", (seqs, width, length), LOW), ("blocks", (blocks, width, LANES), LOW)]
    scratch += [(name + "_box", shapes[name], FLOAT) for name in big]
    sems = [("bsem", blocks // 4), ("insem", seqs), ("outsem", seqs + len(big))]
    names = [i[0] for i in ins] + [o[0] for o in outs] + [s[0] for s in scratch] + [s[0] for s in sems]
    return pl.pallas_call(
        functools.partial(finish_kernel, names, seqs),
        out_shape=tuple(jax.ShapeDtypeStruct(o[1], o[2]) for o in outs),
        in_specs=[i[2] for i in ins],
        out_specs=tuple(o[3] for o in outs),
        scratch_shapes=[pltpu.VMEM(s[1], s[2]) for s in scratch] + [pltpu.SemaphoreType.DMA((s[1],)) for s in sems],
        compiler_params=pltpu.CompilerParams(vmem_limit_bytes=VMEM_MOST),
        name="finish",
    )(*[i[1] for i in ins])


def kernels_fit(tokens, query_weight, key_weight, gate_weight, picks):
    seqs = tokens.shape[0]
    slots = tuple(p.shape[-1] for p in picks)
    return (
        seqs == 4
        and slots == (TILE, TILE // 2, TILE // 4)
        and query_weight.shape == (ROWS, ROWS)
        and key_weight.shape[1] == ROWS // 3
        and gate_weight.shape[1] % 256 == 0
    )


def with_kernels(tokens, weights, router, out_grad, doc_lengths, picks, routes):
    groups, replicas = lax.axis_size("grp"), lax.axis_size("rep")
    (gain_one, query, key, value, output, gain_two, gate, up, down) = weights
    tokens, out_grad = (v.transpose(0, 2, 1) for v in (tokens, out_grad))
    key, value, down = key.T, value.T, down.T
    out_state, grad_rows, places, small, packed = block_call(
        tokens,
        (gain_one[None], query, key, value, output, gain_two[None], gate, up, down, router),
        out_grad, doc_lengths, picks, routes,
    )
    if groups * replicas > 1:
        packed, small = all_reduce(packed, small, groups, replicas)
    shapes = {
        "query": query.shape, "key": key.shape, "value": value.shape, "output": output.shape,
        "gate": gate.shape, "up": up.shape, "down": down.shape,
    }
    done = finish_call(out_grad, grad_rows, places, packed, small, shapes)
    (grad_tokens, query, key, value, output, gate, up, down, gain_one, gain_two, router) = done
    return (
        out_state.transpose(0, 2, 1), grad_tokens.transpose(0, 2, 1), gain_one[0], query, key.T, value.T,
        output, gain_two[0], gate, up, down.T, router,
    )


def per_device(
    tokens,
    attention_gain,
    query_weight,
    key_weight,
    value_weight,
    output_weight,
    feed_gain,
    gate_weight,
    up_weight,
    down_weight,
    router,
    out_grad,
    doc_lengths,
    picks_first,
    picks_second,
    picks_third,
    routes,
):
    seq_count, seq_len, model_width = tokens.shape
    tables = (picks_first, picks_second, picks_third)
    if kernels_fit(tokens, query_weight, key_weight, gate_weight, tables):
        weights = (
            attention_gain, query_weight, key_weight, value_weight, output_weight,
            feed_gain, gate_weight, up_weight, down_weight,
        )
        return with_kernels(tokens, weights, router, out_grad, doc_lengths, tables, routes)
    own_bucket = lax.axis_index("grp")
    weights = (
        attention_gain.astype(jnp.float32),
        query_weight,
        key_weight,
        value_weight,
        output_weight,
        feed_gain.astype(jnp.float32),
        gate_weight,
        up_weight,
        down_weight,
    )
    router_rows = router.astype(jnp.float32)
    lengths = jnp.take(doc_lengths, own_bucket, axis=0)
    doc_ends = jnp.cumsum(lengths, axis=-1)
    counts = jnp.take(routes, own_bucket, axis=0)[:, :, 0]
    seq_positions = jnp.arange(seq_len, dtype=jnp.int32)
    picks = [jnp.take(t, own_bucket, axis=0) for t in (picks_first, picks_second, picks_third)]
    actives = [
        jnp.arange(p.shape[-1])[None, :] < counts[:, r][:, None] for r, p in enumerate(picks)
    ]
    selectors = []
    for r in range(NREC):
        outer = jnp.broadcast_to(seq_positions[None], (seq_count, seq_len)) if r == 0 else picks[r - 1]
        hit = (picks[r][:, :, None] == outer[:, None, :]) & actives[r][:, :, None]
        if r > 0:
            hit = hit & actives[r - 1][:, None, :]
        selectors.append(hit.astype(jnp.bfloat16))
    touched = jnp.any(selectors[0] > 0, axis=1)
    stored = []
    states = []
    rows_now = jnp.einsum("sjp,spd->sjd", selectors[0], tokens, preferred_element_type=jnp.float32)
    for r in range(NREC):
        picked_rows = rows_now
        active = actives[r]
        gate_values = jax.nn.sigmoid(jnp.sum(picked_rows * router_rows[r], axis=-1))
        rows_low = picked_rows.astype(jnp.bfloat16)
        starts = jnp.sum(
            jnp.where(doc_ends[:, None, :] <= picks[r][..., None], lengths[:, None, :], 0), axis=-1
        )
        allowed = attention_mask(jnp.zeros_like(picks[r]), starts, picks[r], active)
        change, log_total = block_forward(rows_low, allowed, picks[r], weights)
        change_rows = change.astype(jnp.bfloat16).astype(jnp.float32).reshape(picked_rows.shape)
        stored.append((picked_rows, gate_values, rows_low, allowed, change_rows, log_total))
        update = gate_values[..., None] * change_rows * active[..., None].astype(jnp.float32)
        states.append(picked_rows + update)
        if r + 1 < NREC:
            rows_now = pick_rows(states[r], selectors[r + 1])
    final = states[-1]
    for r in (1, 0):
        inside = jnp.any(selectors[r + 1] > 0, axis=1)
        parts = exact_parts(final)
        spread = sum(
            jnp.einsum("sjp,sjd->spd", selectors[r + 1], part, preferred_element_type=jnp.float32)
            for part in parts
        )
        final = jnp.where(inside[..., None], spread, states[r])
    placed = jnp.einsum(
        "sjp,sjd->spd", selectors[0], final.astype(jnp.bfloat16), preferred_element_type=jnp.float32
    ).astype(jnp.bfloat16)
    out_state = jnp.where(touched[..., None], placed, tokens)

    grads = [jnp.einsum("sjp,spd->sjd", selectors[0], out_grad, preferred_element_type=jnp.float32)]
    for r in (1, 2):
        grads.append(
            jnp.einsum(
                "sjp,spd->sjd",
                selectors[r],
                grads[-1].astype(jnp.bfloat16),
                preferred_element_type=jnp.float32,
            )
        )
    grad_totals = tuple((jnp.zeros(weight_item.shape, jnp.float32) for weight_item in weights))
    router_terms = [None] * NREC
    for r in (2, 1, 0):
        picked_rows, gate_values, rows_low, allowed, change_rows, log_total = stored[r]
        row_grad = grads[r]
        active_float = actives[r].astype(jnp.float32)
        change_grad = (gate_values[..., None] * row_grad * active_float[..., None]).astype(
            jnp.bfloat16
        )
        logit_grad = (
            jnp.sum(row_grad * change_rows, axis=-1)
            * active_float
            * gate_values
            * (1.0 - gate_values)
        )
        router_terms[r] = jnp.sum(logit_grad[..., None] * picked_rows, axis=(0, 1))
        rows_grad, grad_terms = block_backward(
            rows_low, allowed, picks[r], log_total, change_grad, weights
        )
        grad_totals = tuple(
            (running + fresh_term for running, fresh_term in zip(grad_totals, grad_terms))
        )
        sent_grad = rows_grad.astype(jnp.bfloat16).astype(jnp.float32).reshape(row_grad.shape)
        total = (logit_grad[..., None] * router_rows[r] + sent_grad) * active_float[..., None]
        grads[r] = row_grad + total
        extra = total if r == 2 else extra + total
        if r > 0:
            extra = place_rows(jnp.zeros_like(grads[r - 1]), selectors[r], extra)
            grads[r - 1] = grads[r - 1] + extra
    placed_grad = jnp.einsum(
        "sjp,sjd->spd", selectors[0], grads[0].astype(jnp.bfloat16), preferred_element_type=jnp.float32
    ).astype(jnp.bfloat16)
    grad_tokens = jnp.where(touched[..., None], placed_grad, out_grad)
    router_grad = jnp.stack(router_terms, 0)
    sums = sum_gradients(grad_totals, router_grad)
    return (out_state, grad_tokens) + tuple(sums)


def solution(mesh):
    placed = (
        P(("grp", "rep"), None, None),
        P(),
        P(),
        P(),
        P(),
        P(),
        P(),
        P(),
        P(),
        P(),
        P(),
        P(("grp", "rep"), None, None),
        P(None, "rep", None),
        P(None, "rep", None),
        P(None, "rep", None),
        P(None, "rep", None),
        P(None, "rep", None, None),
    )
    return jax.shard_map(
        per_device,
        mesh=mesh,
        in_specs=placed,
        out_specs=(
            P(("grp", "rep"), None, None),
            P(("grp", "rep"), None, None),
            P(),
            P(),
            P(),
            P(),
            P(),
            P(),
            P(),
            P(),
            P(),
            P(),
        ),
        check_vma=False,
    )
```
